32 devices in a mesh: ctx: 8 (over y, x, core), tp: 4 (over z).
Axes of the slice: x: 2, y: 2, z: 4, core: 2. Of those that a mesh axis runs over, the one named last changes fastest.
Arguments:
- gate_inner: bfloat16 [4096, 8192], P('ctx', 'tp'), may hold values from -6 to 6
- gate_outer: bfloat16 [4096, 8192], P('ctx', 'tp'), may hold values from -6 to 6
- hyena_value: bfloat16 [4096, 8192], P('ctx', 'tp'), may hold values from -6 to 6
- decay_rate: float32 [512, 16], P('tp'), may hold values from 1.2207031e-05 to 0.07
- residue: float32 [512, 16], P('tp'), may hold values from -1 to 1
- skip_gain: float32 [8192], P('tp'), may hold values from 0.5 to 1.5
- filter_index: int32 [512], P('tp'), may hold values from 0 to 511
- query_rows: bfloat16 [4096, 8192], P('ctx', 'tp'), may hold values from -8 to 8
- key_rows: bfloat16 [4096, 8192], P('ctx', 'tp'), may hold values from -8 to 8
- value_rows: bfloat16 [4096, 8192], P('ctx', 'tp'), may hold values from -6 to 6
Outputs:
- hyena_output: bfloat16 [4096, 8192], P('ctx', 'tp')
- attention_output: bfloat16 [4096, 8192], P('ctx', 'tp')
The draws below stay inside these ranges and needn't reach their ends.
All inputs are finite; a program needn't handle non-finite values.
Results may differ from the reference program's by a relative error of at most 0.012.
Values may be sent and summed in bfloat16 or wider, within the bound.
No kernel may reach another device: no remote copies, remote signals or barrier semaphores. Data moves between devices by JAX's collectives and lax.ppermute only.
A program may use at most 192 MiB of HBM per device.

```python
import math
import jax
import jax.numpy as jnp
from jax import lax

D = 8192
HEADS = 64
HEAD_DIM = 128
FILTERS = 512
GROUP = 16
POLES = 16
SEQ = 4096
CGROUPS = 512


def filter_modes(key):
    base_key = jax.random.fold_in(key, 11)
    key_mask, key_slow, key_fast, key_sign = jax.random.split(base_key, 4)
    shape_modes = (FILTERS, POLES)
    slow_share = 0.5
    slow_poles = jax.random.uniform(key_mask, shape_modes) < slow_share
    slow_values = jnp.exp(jax.random.uniform(key_slow, shape_modes, minval=math.log(0.05 / SEQ), maxval=math.log(2.0 / SEQ)))
    fast_values = jnp.exp(jax.random.uniform(key_fast, shape_modes, minval=math.log(1.0 / 40.0), maxval=math.log(1.0 / 15.0)))
    decay_values = jnp.where(slow_poles, slow_values, fast_values).astype(jnp.float32)
    reach = jnp.minimum(0.5 / decay_values, 0.5 * SEQ)
    normals = jnp.clip(jax.random.normal(key_sign, shape_modes), -6.0, 6.0)
    residues = (normals / jnp.sqrt(POLES * reach)).astype(jnp.float32)
    return (decay_values, residues)


def draw_decay_rate(key, part):
    return filter_modes(key)[0]


def draw_residue(key, part):
    return filter_modes(key)[1]


def query_key(key):
    base_key = jax.random.fold_in(key, 23)
    key_query, key_keys = jax.random.split(base_key, 2)
    queries = jnp.clip(jax.random.normal(key_query, (SEQ, D)), -6.0, 6.0)
    keys_drawn = jnp.clip(jax.random.normal(key_keys, (SEQ, D)), -6.0, 6.0)
    return (queries.astype(jnp.float32), keys_drawn.astype(jnp.float32))


def draw_query_rows(key, part):
    return query_key(key)[0].astype(jnp.bfloat16)


def draw_key_rows(key, part):
    return query_key(key)[1].astype(jnp.bfloat16)


def place_ends(values, key, low, top_value):
    spot = [jax.random.randint(jax.random.fold_in(key, axis), (), 0, length) for axis, length in enumerate(values.shape)]
    main_axis = values.shape.index(max(values.shape))
    next_to = spot[:main_axis] + [(spot[main_axis] + 1) % values.shape[main_axis]] + spot[main_axis + 1:]
    return values.at[tuple(spot)].set(low).at[tuple(next_to)].set(top_value)


def shard_levels(rng, dims, shards, smallest, high):
    def one(dim, parts):
        draws = jax.random.uniform(jax.random.fold_in(jax.random.fold_in(rng, 6), dim), (parts,), jnp.float32, smallest / len(shards), high / len(shards))
        return jnp.repeat(jnp.exp(draws), dims[dim] // parts).reshape((-1,) + (1,) * (len(dims) - dim - 1))

    gain = one(*shards[0])
    for cut in shards[1:]:
        gain = gain * one(*cut)
    return gain


def centred(own_key, extent, width, most, shards=(), kind=jnp.bfloat16):
    gain = shard_levels(own_key, extent, shards, -0.22, 0.18) if shards else 1.0
    drawn = jax.random.normal(own_key, extent, jnp.float32) * width * gain
    return jnp.minimum(jnp.maximum(drawn, -most), most).astype(kind)


def setup_inputs(seed: int = 0) -> dict:
    splits = jax.random.split(jax.random.key(seed), 11)
    gate_inner = centred(splits[0], (SEQ, D), 1.0, 6.0, ((0, 8), (1, 4)))
    gate_outer = centred(splits[1], (SEQ, D), 1.0, 6.0, ((0, 8), (1, 4)))
    hyena_value = centred(splits[2], (SEQ, D), 1.0, 6.0, ((0, 8), (1, 4)))
    decay_rate = draw_decay_rate(jax.random.fold_in(splits[10], 71), 0)
    residue = draw_residue(jax.random.fold_in(splits[10], 71), 0)
    skip_gain = jnp.clip(0.5 + 1.0 * jax.random.uniform(splits[5], (D,), jnp.float32) ** shard_levels(splits[5], (D,), ((0, 4),), -0.2, 0.2), 0.5, 1.5)
    filter_index = place_ends(jax.random.randint(splits[6], (CGROUPS,), 0, FILTERS), jax.random.fold_in(splits[6], 1), 0, FILTERS - 1).astype(jnp.int32)
    query_rows = draw_query_rows(jax.random.fold_in(splits[10], 71), 0)
    key_rows = draw_key_rows(jax.random.fold_in(splits[10], 71), 0)
    value_rows = centred(splits[9], (SEQ, D), 1.0, 6.0, ((0, 8), (1, 4)))
    return {"gate_inner": gate_inner, "gate_outer": gate_outer, "hyena_value": hyena_value, "decay_rate": decay_rate, "residue": residue, "skip_gain": skip_gain, "filter_index": filter_index, "query_rows": query_rows, "key_rows": key_rows, "value_rows": value_rows}


def filter_row(params):
    decay_values, residues = params
    lag_values = jnp.arange(SEQ).astype(jnp.float32)
    return lax.optimization_barrier(jnp.sum(residues[:, None] * jnp.exp(-decay_values[:, None] * lag_values[None, :]), axis=0))

def hyena_reference(gate_inner, gate_outer, hyena_value, decay_rate, residue, skip_gain, filter_index):
    product = (gate_inner.astype(jnp.float32) * hyena_value.astype(jnp.float32)).astype(jnp.bfloat16)
    carried = lax.optimization_barrier(product).astype(jnp.float32)
    filter_taps = lax.map(filter_row, (decay_rate, residue))
    chosen = jnp.repeat(filter_taps[filter_index], GROUP, axis=0).T
    fft_size = 2 * SEQ
    spectrum = jnp.fft.rfft(carried, n=fft_size, axis=0) * jnp.fft.rfft(chosen, n=fft_size, axis=0)
    convolved = jnp.fft.irfft(spectrum, n=fft_size, axis=0)[:SEQ] + skip_gain[None, :] * carried
    return (gate_outer.astype(jnp.float32) * convolved).astype(jnp.bfloat16)

def attention_reference(query_rows, key_rows, value_rows):
    block_rows = min(512, SEQ)
    head_step = min(8, HEADS)
    score_scale = 1.0 / math.sqrt(HEAD_DIM)
    queries = query_rows.astype(jnp.float32).reshape(SEQ, HEADS, HEAD_DIM)
    keys_all = key_rows.astype(jnp.float32).reshape(SEQ, HEADS, HEAD_DIM)
    values_all = value_rows.astype(jnp.float32).reshape(SEQ, HEADS, HEAD_DIM)
    blocks_done = []
    for first_row in range(0, SEQ, block_rows):
        last_row = first_row + block_rows
        visible = jnp.arange(first_row, last_row)[:, None] >= jnp.arange(last_row)[None, :]
        head_parts = []
        for head_first in range(0, HEADS, head_step):
            head_last = head_first + head_step
            scores = jnp.einsum('thd,shd->hts', queries[first_row:last_row, head_first:head_last], keys_all[:last_row, head_first:head_last], precision=lax.Precision.HIGHEST) * score_scale
            masked = jnp.where(visible[None], scores, -jnp.inf)
            row_max = lax.optimization_barrier(jnp.max(masked, axis=2, keepdims=True))
            weights = jnp.where(visible[None], jnp.exp(scores - row_max), 0.0)
            row_total = lax.optimization_barrier(jnp.sum(weights, axis=2))
            rounded = lax.optimization_barrier(weights.astype(jnp.bfloat16)).astype(jnp.float32)
            summed = jnp.einsum('hts,shd->thd', rounded, values_all[:last_row, head_first:head_last], precision=lax.Precision.HIGHEST)
            head_parts.append(summed / row_total.T[:, :, None])
        blocks_done.append(jnp.concatenate(head_parts, axis=1))
    return jnp.concatenate(blocks_done, axis=0).reshape(SEQ, D).astype(jnp.bfloat16)

def reference(gate_inner, gate_outer, hyena_value, decay_rate, residue, skip_gain, filter_index, query_rows, key_rows, value_rows):
    hyena_output = hyena_reference(gate_inner, gate_outer, hyena_value, decay_rate, residue, skip_gain, filter_index)
    attention_output = attention_reference(query_rows, key_rows, value_rows)
    return (hyena_output, attention_output)
```

```python
import functools
import math

import jax
import jax.numpy as jnp
from jax import lax
from jax.experimental import pallas as pl
from jax.experimental.pallas import tpu as pltpu
from jax.sharding import PartitionSpec as P

HEAD_DIM = 128
GROUP = 16
LANES = 128
CHUNK = 128
TILE_GROUPS = LANES // GROUP

floor_score = -1e30
LOG2E = 1.4426950408889634


F32 = jnp.float32
BF16 = jnp.bfloat16
LAST = (((1,), (1,)), ((), ()))
FIRST = (((0,), (0,)), ((), ()))
PLAIN = (((1,), (0,)), ((), ()))


def mxu(a, b, dims):
    return lax.dot_general(a, b, dims, preferred_element_type=F32)


def halves(a):
    high = a.astype(BF16)
    return high, (a - high.astype(F32)).astype(BF16)


def mxu3(a, b, dims):
    a_high, a_low = halves(a)
    b_high, b_low = halves(b)
    return mxu(a_high, b_high, dims) + (mxu(a_low, b_high, dims) + mxu(a_high, b_low, dims))


def iota(shape, axis):
    return lax.broadcasted_iota(jnp.int32, shape, axis)


def same_group():
    rows, cols = iota((LANES, LANES), 0), iota((LANES, LANES), 1)
    return (rows // GROUP) == (cols // GROUP)


def state_kernel(gate_ref, value_ref, rate_ref, state_ref):
    rows = gate_ref.shape[0]
    carried = (gate_ref[...].astype(F32) * value_ref[...].astype(F32)).astype(BF16)
    left = (rows - iota((rows, LANES), 0)).astype(F32)
    weight_high, weight_low = halves(jnp.exp(-left * rate_ref[0]))
    full = mxu(carried, weight_high, FIRST) + mxu(carried, weight_low, FIRST)
    kept = jnp.where(same_group(), full, 0.0).astype(BF16)
    pick = (iota((GROUP, LANES), 1) % GROUP == iota((GROUP, LANES), 0)).astype(BF16)
    state_ref[0] = mxu(pick, kept, PLAIN).astype(BF16)


def hyena_kernel(gate_ref, outer_ref, value_ref, rate_ref, residue_ref, skip_ref, state_ref, out_ref):
    rows = gate_ref.shape[0]
    chunks = rows // CHUNK
    rate, residue, skip = rate_ref[0], residue_ref[0], skip_ref[0]
    step = iota((CHUNK, LANES), 0).astype(F32)
    grown = jnp.exp((step - CHUNK // 2) * rate)
    shrunk = residue * jnp.exp((CHUNK // 2 - step) * rate)
    from_start = residue * jnp.exp(-step * rate)
    to_end_high, to_end_low = halves(jnp.exp((step - CHUNK) * rate))
    decay = jnp.exp(-CHUNK * rate)
    lane_group = iota((CHUNK, LANES), 1) // GROUP
    grown_high, grown_low = halves(grown)
    zero = jnp.zeros((), BF16)
    spread_high = jnp.concatenate(
        [jnp.where(lane_group == g, grown_high, zero) for g in range(TILE_GROUPS)], axis=0
    )
    spread_low = jnp.concatenate(
        [jnp.where(lane_group == g, grown_low, zero) for g in range(TILE_GROUPS)], axis=0
    )
    shrunk_high, shrunk_low = halves(shrunk)
    taps = mxu(shrunk_high, spread_high, LAST) + (
        mxu(shrunk_low, spread_high, LAST) + mxu(shrunk_high, spread_low, LAST)
    )
    shape = (CHUNK, TILE_GROUPS * CHUNK)
    causal = iota(shape, 0) >= iota(shape, 1) % CHUNK
    toeplitz = jnp.where(causal, taps, 0.0).astype(BF16)
    carried = (gate_ref[...].astype(F32) * value_ref[...].astype(F32)).astype(BF16)
    pieces = [carried[b * CHUNK : (b + 1) * CHUNK] for b in range(chunks)]
    blocks = jnp.concatenate(
        [
            jnp.concatenate([jnp.where(lane_group == g, piece, zero) for piece in pieces], axis=1)
            for g in range(TILE_GROUPS)
        ],
        axis=0,
    )
    inside = mxu(toeplitz, blocks, PLAIN)
    mask = same_group()
    pick = (iota((LANES, GROUP), 0) % GROUP == iota((LANES, GROUP), 1)).astype(BF16)
    state = jnp.where(mask, mxu(pick, state_ref[0], PLAIN), 0.0)
    for b in range(chunks):
        piece = pieces[b]
        earlier = mxu3(from_start, state, LAST)
        convolved = inside[:, b * LANES : (b + 1) * LANES] + earlier + skip * piece.astype(F32)
        gate = outer_ref[b * CHUNK : (b + 1) * CHUNK, :].astype(F32)
        out_ref[b * CHUNK : (b + 1) * CHUNK, :] = (gate * convolved).astype(BF16)
        if b + 1 < chunks:
            fresh = mxu(piece, to_end_high, FIRST) + mxu(piece, to_end_low, FIRST)
            state = state * decay + jnp.where(mask, fresh, 0.0)


def hyena_body(gate_inner, gate_outer, hyena_value, decay_rate, residue, skip_gain, filter_index, mesh):
    row_count, chan_count = gate_inner.shape
    tiles = chan_count // LANES
    ctx_size, tp_size = mesh.shape["ctx"], mesh.shape["tp"]
    modes = jnp.concatenate([decay_rate, residue], axis=1)
    filters, width = modes.shape
    place = lax.axis_index("tp")
    bank = jnp.zeros((tp_size * filters, width), F32)
    bank = lax.dynamic_update_slice(bank, modes, (place * filters, 0))
    if tp_size <= 4:
        for shift in range(1, tp_size):
            other = lax.ppermute(modes, "tp", [(i, (i + shift) % tp_size) for i in range(tp_size)])
            owner = (place - shift) % tp_size
            bank = lax.dynamic_update_slice(bank, other, (owner * filters, 0))
    else:
        bank = lax.all_gather(modes, "tp", axis=0, tiled=True)
    chooser = (
        filter_index[:, None] == jnp.arange(tp_size * filters, dtype=jnp.int32)[None, :]
    ).astype(F32)
    local = jnp.dot(chooser, bank, precision=lax.Precision.HIGHEST)
    poles = width // 2
    rate = local[:, :poles].reshape(tiles, 1, LANES)
    local_residue = local[:, poles:].reshape(tiles, 1, LANES)
    skip = skip_gain.reshape(tiles, 1, LANES)

    wide = pl.BlockSpec((row_count, LANES), lambda i: (0, i))
    row = pl.BlockSpec((1, 1, LANES), lambda i: (i, 0, 0))
    small = pl.BlockSpec((1, GROUP, LANES), lambda i: (i, 0, 0))
    state = pl.pallas_call(
        state_kernel,
        grid=(tiles,),
        in_specs=[wide, wide, row],
        out_specs=small,
        out_shape=jax.ShapeDtypeStruct((tiles, GROUP, LANES), BF16),
        cost_estimate=pl.CostEstimate(
            flops=4 * row_count * chan_count * LANES,
            bytes_accessed=4 * row_count * chan_count,
            transcendentals=row_count * chan_count,
        ),
        name="states",
    )(gate_inner, hyena_value, rate)

    def shifted(a, by):
        return lax.ppermute(a, "ctx", [(i, i + by) for i in range(ctx_size - by)])

    step = float(row_count)
    incoming = shifted(state, 1).astype(F32)
    if ctx_size > 2:
        incoming = incoming + shifted(state, 2).astype(F32) * jnp.exp(-rate * step)
    reach = 2
    while reach < ctx_size - 1:
        incoming = incoming + shifted(incoming.astype(BF16), reach).astype(F32) * jnp.exp(
            -rate * (step * reach)
        )
        reach *= 2
    incoming = incoming.astype(BF16)
    return pl.pallas_call(
        hyena_kernel,
        grid=(tiles,),
        in_specs=[wide, wide, wide, row, row, row, small],
        out_specs=wide,
        out_shape=jax.ShapeDtypeStruct((row_count, chan_count), BF16),
        cost_estimate=pl.CostEstimate(
            flops=2 * row_count * chan_count * LANES * 16,
            bytes_accessed=8 * row_count * chan_count,
            transcendentals=row_count * chan_count,
        ),
        name="hyena",
    )(gate_inner, gate_outer, hyena_value, rate, local_residue, skip, incoming)


def flash_kernel(place_ref, *refs, blocks):
    sources, outs = refs[:blocks], refs[blocks : 2 * blocks]
    q_buf, k_buf, v_buf, o_buf, m_buf, acc_buf, sems = refs[2 * blocks :]
    rows = sources[0].shape[0]
    place = place_ref[0]
    copies = []
    for r in range(blocks):
        spot = pl.ds(pl.multiple_of((place ^ r) * rows, rows), rows)
        for j, target in enumerate(
            (q_buf.at[spot], k_buf.at[spot], v_buf.at[spot, pl.ds(0, HEAD_DIM)])
        ):
            copies.append(
                pltpu.make_async_copy(
                    sources[r].at[:, pl.ds(j * HEAD_DIM, HEAD_DIM)], target, sems.at[r, j]
                )
            )
            copies[-1].start()
    v_buf[:, HEAD_DIM:] = jnp.ones((blocks * rows, HEAD_DIM), BF16)
    for copy in copies:
        copy.wait()
    scale = LOG2E / math.sqrt(HEAD_DIM)

    def one_query(i, carry):
        q_rows = pl.ds(pl.multiple_of(i * rows, rows), rows)
        query = q_buf[q_rows, :]
        m_buf[...] = jnp.full(m_buf.shape, floor_score, F32)
        acc_buf[...] = jnp.zeros(acc_buf.shape, F32)

        def visit(j, masked):
            k_rows = pl.ds(pl.multiple_of(j * rows, rows), rows)
            scores = mxu(query, k_buf[k_rows, :], LAST)
            if masked:
                scores = jnp.where(
                    iota((rows, rows), 0) >= iota((rows, rows), 1), scores, floor_score
                )
            old = m_buf[:, :1]
            newest = jnp.maximum(old, jnp.max(scores, axis=1, keepdims=True) * scale)
            weights = jnp.exp2(scores * scale - newest).astype(BF16)
            factor = jnp.exp2(old - newest)
            m_buf[...] = jnp.broadcast_to(newest, m_buf.shape)
            acc_buf[...] = acc_buf[...] * factor + mxu(weights, v_buf[k_rows, :], PLAIN)

        def plain(j, carry):
            visit(j, False)
            return carry

        lax.fori_loop(0, i, plain, 0)
        visit(i, True)
        total = acc_buf[...]
        o_buf[q_rows, :] = (total[:, :HEAD_DIM] / total[:, HEAD_DIM:]).astype(BF16)
        return carry

    lax.fori_loop(0, blocks, one_query, 0)
    for r in range(blocks):
        spot = pl.ds(pl.multiple_of((place ^ r) * rows, rows), rows)
        outs[r][...] = o_buf[spot, :]


def flash(place, sources):
    blocks, rows = len(sources), sources[0].shape[0]
    total = blocks * rows
    pairs = total * (total + rows) // 2
    return pl.pallas_call(
        functools.partial(flash_kernel, blocks=blocks),
        in_specs=[pl.BlockSpec(memory_space=pltpu.SMEM)]
        + [pl.BlockSpec(memory_space=pl.ANY)] * blocks,
        out_specs=[pl.BlockSpec(memory_space=pltpu.VMEM)] * blocks,
        out_shape=[jax.ShapeDtypeStruct((rows, HEAD_DIM), BF16)] * blocks,
        scratch_shapes=[
            pltpu.VMEM((total, HEAD_DIM), BF16),
            pltpu.VMEM((total, HEAD_DIM), BF16),
            pltpu.VMEM((total, 2 * HEAD_DIM), BF16),
            pltpu.VMEM((total, HEAD_DIM), BF16),
            pltpu.VMEM((rows, HEAD_DIM), F32),
            pltpu.VMEM((rows, 2 * HEAD_DIM), F32),
            pltpu.SemaphoreType.DMA((blocks, 3)),
        ],
        cost_estimate=pl.CostEstimate(
            flops=8 * pairs * HEAD_DIM, bytes_accessed=8 * total * HEAD_DIM, transcendentals=pairs
        ),
        name="flash",
    )(place, *sources)


def join_kernel(place_ref, *refs, blocks, heads):
    parts, out_ref = refs[: blocks * heads], refs[blocks * heads]
    sems = refs[blocks * heads + 1]
    place = place_ref[0]
    copies = []
    for r in range(blocks):
        for h in range(heads):
            column = pl.multiple_of(((place ^ r) * heads + h) * HEAD_DIM, HEAD_DIM)
            copies.append(
                pltpu.make_async_copy(
                    parts[r * heads + h], out_ref.at[:, pl.ds(column, HEAD_DIM)], sems.at[r, h]
                )
            )
            copies[-1].start()
    for copy in copies:
        copy.wait()


def exchange_attention(query_rows, key_rows, value_rows, ctx_size):
    row_count, width_cols = query_rows.shape
    heads = width_cols // HEAD_DIM // ctx_size
    place = lax.axis_index("ctx")
    where = place.astype(jnp.int32).reshape(1)

    def pairs(r):
        return [(i, i ^ r) for i in range(ctx_size)]

    def packed(h, r):
        column = ((place ^ r) * heads + h) * HEAD_DIM
        return jnp.concatenate(
            [
                lax.dynamic_slice(a, (0, column), (row_count, HEAD_DIM))
                for a in (query_rows, key_rows, value_rows)
            ],
            axis=1,
        )

    order = sorted(range(ctx_size), key=lambda r: (-bin(r >> 1).count("1"), r))
    got = []
    for h in range(heads):
        mine = {}
        for r in order:
            part = packed(h, r)
            mine[r] = lax.ppermute(part, "ctx", pairs(r)) if r else part
        got.append([mine[r] for r in range(ctx_size)])
    backs = []
    for h in range(heads):
        results = flash(where, got[h])
        backs.append(
            [lax.ppermute(a, "ctx", pairs(r)) if r else a for r, a in enumerate(results)]
        )
    parts = [backs[h][r] for r in range(ctx_size) for h in range(heads)]
    return pl.pallas_call(
        functools.partial(join_kernel, blocks=ctx_size, heads=heads),
        in_specs=[pl.BlockSpec(memory_space=pltpu.SMEM)]
        + [pl.BlockSpec(memory_space=pltpu.VMEM)] * len(parts),
        out_specs=pl.BlockSpec(memory_space=pl.ANY),
        out_shape=jax.ShapeDtypeStruct((row_count, width_cols), BF16),
        scratch_shapes=[pltpu.SemaphoreType.DMA((ctx_size, heads))],
        name="join",
    )(where, *parts)


def row_steps(folded, members, handler, span_rows):
    total_rows = members[0].shape[0]
    block_count = total_rows // span_rows
    stacked = tuple(
        (member.reshape((block_count, span_rows) + member.shape[1:]) for member in members)
    )

    def advance(running, element):
        position, pieces = element
        return (handler(running, pieces, position * span_rows), None)

    folded, ignored = lax.scan(advance, folded, (jnp.arange(block_count, dtype=jnp.int32), stacked))
    return folded


def gather_attention(query_rows, key_rows, value_rows):
    row_count, width_cols = query_rows.shape
    head_count = width_cols // HEAD_DIM
    queries = query_rows.reshape(row_count, head_count, HEAD_DIM)
    score_scale = 1.0 / math.sqrt(HEAD_DIM)
    own_rows = lax.axis_index("ctx") * row_count + jnp.arange(row_count, dtype=jnp.int32)

    def attend(folded, pieces, first_row):
        running_max, running_total, summed = folded
        block_rows = pieces[0].shape[0]
        keys_now = pieces[0].reshape(block_rows, head_count, HEAD_DIM)
        values_now = pieces[1].reshape(block_rows, head_count, HEAD_DIM)
        scores = (
            jnp.einsum("thd,shd->hts", queries, keys_now, preferred_element_type=jnp.float32)
            * score_scale
        )
        key_positions = first_row + jnp.arange(block_rows, dtype=jnp.int32)
        visible = own_rows[:, None] >= key_positions[None, :]
        masked = jnp.where(visible[None], scores, floor_score)
        newest = jnp.maximum(running_max, jnp.max(masked, axis=2))
        weights = jnp.where(visible[None], jnp.exp(scores - newest[:, :, None]), 0.0)
        factor = jnp.exp(running_max - newest)
        running_total = running_total * factor + jnp.sum(weights, axis=2)
        update = jnp.einsum(
            "hts,shd->thd",
            weights.astype(jnp.bfloat16),
            values_now,
            preferred_element_type=jnp.float32,
        )
        summed = summed * factor.T[:, :, None] + update
        return (newest, running_total, summed)

    initial = (
        jnp.full((head_count, row_count), floor_score, jnp.float32),
        jnp.zeros((head_count, row_count), jnp.float32),
        jnp.zeros((row_count, head_count, HEAD_DIM), jnp.float32),
    )
    running_max, running_total, summed = row_steps(
        initial,
        (
            lax.all_gather(key_rows, "ctx", axis=0, tiled=True),
            lax.all_gather(value_rows, "ctx", axis=0, tiled=True),
        ),
        attend,
        512,
    )
    result = summed / running_total.T[:, :, None]
    return result.reshape(row_count, width_cols).astype(jnp.bfloat16)


def attention_body(query_rows, key_rows, value_rows, mesh):
    ctx_size = mesh.shape["ctx"]
    head_count = query_rows.shape[1] // HEAD_DIM
    if head_count % ctx_size == 0 and ctx_size & (ctx_size - 1) == 0:
        return exchange_attention(query_rows, key_rows, value_rows, ctx_size)
    return gather_attention(query_rows, key_rows, value_rows)


def solution(mesh):
    def body(
        gate_inner,
        gate_outer,
        hyena_value,
        decay_rate,
        residue,
        skip_gain,
        filter_index,
        query_rows,
        key_rows,
        value_rows,
    ):
        attention_output = attention_body(query_rows, key_rows, value_rows, mesh)
        hyena_output = hyena_body(
            gate_inner, gate_outer, hyena_value, decay_rate, residue, skip_gain, filter_index, mesh
        )
        return (hyena_output, attention_output)

    in_specs = (
        P("ctx", "tp"),
        P("ctx", "tp"),
        P("ctx", "tp"),
        P("tp", None),
        P("tp", None),
        P("tp"),
        P("tp"),
        P("ctx", "tp"),
        P("ctx", "tp"),
        P("ctx", "tp"),
    )
    out_specs = (P("ctx", "tp"), P("ctx", "tp"))
    return jax.shard_map(body, mesh=mesh, in_specs=in_specs, out_specs=out_specs, check_vma=False)
```

```python
import functools
import math

import jax
import jax.numpy as jnp
from jax import lax
from jax.experimental import pallas as pl
from jax.experimental.pallas import tpu as pltpu
from jax.sharding import PartitionSpec as P

HEAD_DIM = 128
GROUP = 16
LANES = 128
CHUNK = 128
TILE_GROUPS = LANES // GROUP
STEP_TILES = 4

floor_score = -1e30
LOG2E = 1.4426950408889634


F32 = jnp.float32
BF16 = jnp.bfloat16
LAST = (((1,), (1,)), ((), ()))
FIRST = (((0,), (0,)), ((), ()))
PLAIN = (((1,), (0,)), ((), ()))


def mxu(a, b, dims):
    return lax.dot_general(a, b, dims, preferred_element_type=F32)


def halves(a):
    high = a.astype(BF16)
    return high, (a - high.astype(F32)).astype(BF16)


def iota(shape, axis):
    return lax.broadcasted_iota(jnp.int32, shape, axis)


def same_group():
    rows, cols = iota((LANES, LANES), 0), iota((LANES, LANES), 1)
    return (rows // GROUP) == (cols // GROUP)


def carried_pieces(gate_ref, value_ref, lanes):
    rows = gate_ref.shape[0]
    carried = (gate_ref[:, lanes].astype(F32) * value_ref[:, lanes].astype(F32)).astype(BF16)
    return [carried[b * CHUNK : (b + 1) * CHUNK] for b in range(rows // CHUNK)]


def chunk_states(pieces, rate, step, mask):
    ends = jnp.concatenate(halves(jnp.exp((step - CHUNK) * rate)), axis=1)
    full = mxu(jnp.concatenate(pieces, axis=1), ends, FIRST)
    full = full[:, :LANES] + full[:, LANES:]
    return [
        jnp.where(mask, full[b * LANES : (b + 1) * LANES], 0.0) for b in range(len(pieces))
    ]


def spread_states(states, shrinking):
    state_high, state_low = halves(jnp.concatenate(states, axis=0))
    return mxu(
        jnp.concatenate(shrinking, axis=1),
        jnp.concatenate([state_high, state_high], axis=1),
        LAST,
    ) + mxu(shrinking[0], state_low, LAST)


def local_kernel(gate_ref, outer_ref, value_ref, rate_ref, residue_ref, skip_ref, out_ref, state_ref):
    cols = gate_ref.shape[1]
    step = iota((CHUNK, LANES), 0).astype(F32)
    lane_group = iota((CHUNK, LANES), 1) // GROUP
    zero = jnp.zeros((), BF16)
    shape = (CHUNK, TILE_GROUPS * CHUNK)
    causal = iota(shape, 0) >= iota(shape, 1) % CHUNK
    mask = same_group()
    pick = (iota((GROUP, LANES), 1) % GROUP == iota((GROUP, LANES), 0)).astype(BF16)

    def spread(a):
        return jnp.concatenate(
            [jnp.where(lane_group == g, a, zero) for g in range(TILE_GROUPS)], axis=0
        )

    for w in range(cols // LANES):
        lanes = slice(w * LANES, (w + 1) * LANES)
        rate, residue, skip = rate_ref[w], residue_ref[w], skip_ref[w]
        grown_high, grown_low = halves(jnp.exp((step - CHUNK // 2) * rate))
        shrunk = halves(residue * jnp.exp((CHUNK // 2 - step) * rate))
        from_start = halves(residue * jnp.exp(-step * rate))
        decay = jnp.exp(-CHUNK * rate)
        spread_high = spread(grown_high)
        taps = mxu(
            jnp.concatenate(shrunk, axis=1),
            jnp.concatenate([spread_high, spread_high], axis=1),
            LAST,
        ) + mxu(shrunk[0], spread(grown_low), LAST)
        toeplitz = jnp.where(causal, taps, 0.0).astype(BF16)
        pieces = carried_pieces(gate_ref, value_ref, lanes)
        blocks = jnp.concatenate(
            [
                jnp.concatenate(
                    [jnp.where(lane_group == g, piece, zero) for piece in pieces], axis=1
                )
                for g in range(TILE_GROUPS)
            ],
            axis=0,
        )
        inside = mxu(toeplitz, blocks, PLAIN)
        fresh = chunk_states(pieces, rate, step, mask)
        states = [fresh[0]]
        for more in fresh[1:]:
            states.append(states[-1] * decay + more)
        state_ref[w] = mxu(pick, states[-1].astype(BF16), PLAIN).astype(BF16)
        earlier = spread_states(states[:-1], from_start) if len(pieces) > 1 else None
        for b, piece in enumerate(pieces):
            convolved = inside[:, b * LANES : (b + 1) * LANES] + skip * piece.astype(F32)
            if b:
                convolved += earlier[:, (b - 1) * LANES : b * LANES]
            gate = outer_ref[b * CHUNK : (b + 1) * CHUNK, lanes].astype(F32)
            out_ref[b * CHUNK : (b + 1) * CHUNK, lanes] = gate * convolved


def remote_kernel(part_ref, outer_ref, rate_ref, residue_ref, state_ref, out_ref):
    rows, cols = outer_ref.shape
    chunks = rows // CHUNK
    step = iota((CHUNK, LANES), 0).astype(F32)
    mask = same_group()
    pick = (iota((LANES, GROUP), 0) % GROUP == iota((LANES, GROUP), 1)).astype(BF16)
    for w in range(cols // LANES):
        lanes = slice(w * LANES, (w + 1) * LANES)
        rate, residue = rate_ref[w], residue_ref[w]
        decay = jnp.exp(-CHUNK * rate)
        states = [jnp.where(mask, mxu(pick, state_ref[w], PLAIN), 0.0)]
        while len(states) < chunks:
            states.append(states[-1] * decay)
        earlier = spread_states(states, halves(residue * jnp.exp(-step * rate)))
        for b in range(chunks):
            rows_now = slice(b * CHUNK, (b + 1) * CHUNK)
            gate = outer_ref[rows_now, lanes].astype(F32)
            out_ref[rows_now, lanes] = (
                part_ref[rows_now, lanes] + gate * earlier[:, b * LANES : (b + 1) * LANES]
            ).astype(BF16)


def after(value, *earlier):
    return lax.optimization_barrier((value,) + earlier)[0]


def gathered_modes(decay_rate, residue, filter_index, tiles, tp_size, gate):
    modes = jnp.concatenate([decay_rate, residue], axis=1)
    if gate is not None:
        modes = after(modes, gate)
    filters, width = modes.shape
    if tp_size <= 4:
        place = lax.axis_index("tp")
        others = [modes] + [
            lax.ppermute(modes, "tp", [(i, (i + shift) % tp_size) for i in range(tp_size)])
            for shift in range(1, tp_size)
        ]
        bank = jnp.concatenate(others, axis=0)
        owner = filter_index // filters
        wanted = (place - owner) % tp_size * filters + filter_index % filters
    else:
        bank = lax.all_gather(modes, "tp", axis=0, tiled=True)
        wanted = filter_index
    chooser = (wanted[:, None] == jnp.arange(bank.shape[0], dtype=jnp.int32)[None, :]).astype(F32)
    local = jnp.dot(chooser, bank, precision=lax.Precision.HIGHEST)
    poles = width // 2
    return (
        local[:, :poles].reshape(tiles, 1, LANES),
        local[:, poles:].reshape(tiles, 1, LANES),
    )


def hyena_specs(row_count, tiles):
    group = math.gcd(tiles, STEP_TILES)
    return (
        (tiles // group,),
        pl.BlockSpec((row_count, group * LANES), lambda i: (0, i)),
        pl.BlockSpec((group, 1, LANES), lambda i: (i, 0, 0)),
        pl.BlockSpec((group, GROUP, LANES), lambda i: (i, 0, 0)),
    )


def local_part(gate_inner, gate_outer, hyena_value, rate, residue, skip_gain):
    row_count, chan_count = gate_inner.shape
    tiles = chan_count // LANES
    grid, wide, row, small = hyena_specs(row_count, tiles)
    return pl.pallas_call(
        local_kernel,
        grid=grid,
        in_specs=[wide, wide, wide, row, row, row],
        out_specs=[wide, small],
        out_shape=[
            jax.ShapeDtypeStruct((row_count, chan_count), F32),
            jax.ShapeDtypeStruct((tiles, GROUP, LANES), BF16),
        ],
        cost_estimate=pl.CostEstimate(
            flops=2 * row_count * chan_count * LANES * 16,
            bytes_accessed=10 * row_count * chan_count,
            transcendentals=row_count * chan_count,
        ),
        name="local_part",
    )(gate_inner, gate_outer, hyena_value, rate, residue, skip_gain.reshape(tiles, 1, LANES))


def remote_part(part, gate_outer, rate, residue, incoming):
    row_count, chan_count = gate_outer.shape
    tiles = chan_count // LANES
    grid, wide, row, small = hyena_specs(row_count, tiles)
    return pl.pallas_call(
        remote_kernel,
        grid=grid,
        in_specs=[wide, wide, row, row, small],
        out_specs=wide,
        out_shape=jax.ShapeDtypeStruct((row_count, chan_count), BF16),
        cost_estimate=pl.CostEstimate(
            flops=2 * row_count * chan_count * LANES * 3,
            bytes_accessed=8 * row_count * chan_count,
            transcendentals=row_count * chan_count // 4,
        ),
        name="remote_part",
    )(part, gate_outer, rate, residue, incoming)


def shifted(a, by, ctx_size):
    return lax.ppermute(a.astype(BF16), "ctx", [(i, i + by) for i in range(ctx_size - by)])


def scan_join(value, moved, base, rate, rows):
    for k, more in enumerate(moved, 1):
        value = value + more.astype(F32) * jnp.exp(-rate * float(rows * base * k))
    return value


def hyena_plain(gate_inner, gate_outer, hyena_value, modes, skip_gain, ctx_size):
    rate, residue = modes
    rows = gate_inner.shape[0]
    part, state = local_part(gate_inner, gate_outer, hyena_value, rate, residue, skip_gain)
    incoming = shifted(state, 1, ctx_size).astype(F32)
    base = 1
    while base < ctx_size - 1:
        incoming = scan_join(incoming, [shifted(incoming, base, ctx_size)], base, rate, rows)
        base *= 2
    return remote_part(part, gate_outer, rate, residue, incoming.astype(BF16))


def pack_kernel(place_ref, q_ref, k_ref, v_ref, *refs, spots, heads, head):
    outs, (buf, sems, out_sems) = refs[: len(spots)], refs[len(spots) :]
    place = place_ref[0]
    reads = []
    for n, r in enumerate(spots):
        column = pl.multiple_of(((place ^ r) * heads + head) * HEAD_DIM, HEAD_DIM)
        for j, source in enumerate((q_ref, k_ref, v_ref)):
            reads.append(
                pltpu.make_async_copy(
                    source.at[:, pl.ds(column, HEAD_DIM)],
                    buf.at[n, :, pl.ds(j * HEAD_DIM, HEAD_DIM)],
                    sems.at[n, j],
                )
            )
            reads[-1].start()
    writes = []
    for n in range(len(spots)):
        for j in range(3):
            reads[3 * n + j].wait()
        writes.append(pltpu.make_async_copy(buf.at[n], outs[n], out_sems.at[n]))
        writes[-1].start()
    for write in writes:
        write.wait()


def pack(place, arrays, spots, heads, head):
    rows = arrays[0].shape[0]
    shape = (rows, 3 * HEAD_DIM)
    return pl.pallas_call(
        functools.partial(pack_kernel, spots=spots, heads=heads, head=head),
        in_specs=[pl.BlockSpec(memory_space=pltpu.SMEM)]
        + [pl.BlockSpec(memory_space=pl.ANY)] * 3,
        out_specs=[pl.BlockSpec(memory_space=pl.ANY)] * len(spots),
        out_shape=[jax.ShapeDtypeStruct(shape, BF16)] * len(spots),
        scratch_shapes=[
            pltpu.VMEM((len(spots),) + shape, BF16),
            pltpu.SemaphoreType.DMA((len(spots), 3)),
            pltpu.SemaphoreType.DMA((len(spots),)),
        ],
        cost_estimate=pl.CostEstimate(
            flops=0, bytes_accessed=4 * len(spots) * rows * 3 * HEAD_DIM, transcendentals=0
        ),
        name="pack",
    )(place, *arrays)


def flash_kernel(place_ref, *refs, blocks):
    sources, outs = refs[:blocks], refs[blocks : 2 * blocks]
    q_buf, k_buf, v_buf, vt_buf, o_buf, s_buf, m_buf, l_buf, acc_buf, sems = refs[2 * blocks :]
    rows = sources[0].shape[0]
    place = place_ref[0]
    copies = []
    for r in range(blocks):
        spot = pl.ds(pl.multiple_of((place ^ r) * rows, rows), rows)
        for j, target in enumerate((q_buf, k_buf, v_buf)):
            copies.append(
                pltpu.make_async_copy(
                    sources[r].at[:, pl.ds(j * HEAD_DIM, HEAD_DIM)], target.at[spot], sems.at[r, j]
                )
            )
            copies[-1].start()
    for copy in copies:
        copy.wait()
    for j in range(blocks):
        vt_buf[:, j * rows : (j + 1) * rows] = v_buf[j * rows : (j + 1) * rows, :].T
    scale = LOG2E / math.sqrt(HEAD_DIM)

    def score(i, j):
        keys = slice(j * rows, (j + 1) * rows)
        scores = mxu(k_buf[keys, :], q_buf[i * rows : (i + 1) * rows, :], LAST)
        if i == j:
            shape = (rows, rows)
            scores = jnp.where(iota(shape, 1) >= iota(shape, 0), scores, floor_score)
        s_buf[i % 2, keys, :] = scores
        m_buf[i % 2] = jnp.maximum(
            m_buf[i % 2], jnp.max(scores.reshape(rows // 8, 8, rows), axis=0)
        )

    def weigh(i, j, top):
        keys = slice(j * rows, (j + 1) * rows)
        weights = jnp.exp2(s_buf[i % 2, keys, :] * scale - top)
        l_buf[...] += jnp.sum(weights.reshape(rows // 8, 8, rows), axis=0)
        acc_buf[...] += mxu(vt_buf[:, keys], weights.astype(BF16), PLAIN)

    m_buf[...] = jnp.full(m_buf.shape, floor_score, F32)
    score(0, 0)
    for i in range(blocks):
        top = jnp.max(m_buf[i % 2], axis=0, keepdims=True) * scale
        m_buf[(i + 1) % 2] = jnp.full((8, rows), floor_score, F32)
        acc_buf[...] = jnp.zeros(acc_buf.shape, F32)
        l_buf[...] = jnp.zeros(l_buf.shape, F32)
        for j in range(i + 2):
            if j <= i:
                weigh(i, j, top)
            if i + 1 < blocks:
                score(i + 1, j)
        total = jnp.sum(l_buf[...], axis=0, keepdims=True)
        o_buf[i * rows : (i + 1) * rows, :] = (acc_buf[...] / total).T.astype(BF16)
    writes = []
    for r in range(blocks):
        spot = pl.ds(pl.multiple_of((place ^ r) * rows, rows), rows)
        writes.append(pltpu.make_async_copy(o_buf.at[spot], outs[r], sems.at[r, 0]))
        writes[-1].start()
    for write in writes:
        write.wait()


def flash(place, sources):
    blocks, rows = len(sources), sources[0].shape[0]
    total = blocks * rows
    pairs = total * (total + rows) // 2
    return pl.pallas_call(
        functools.partial(flash_kernel, blocks=blocks),
        in_specs=[pl.BlockSpec(memory_space=pltpu.SMEM)]
        + [pl.BlockSpec(memory_space=pl.ANY)] * blocks,
        out_specs=[pl.BlockSpec(memory_space=pl.ANY)] * blocks,
        out_shape=[jax.ShapeDtypeStruct((rows, HEAD_DIM), BF16)] * blocks,
        scratch_shapes=[
            pltpu.VMEM((total, HEAD_DIM), BF16),
            pltpu.VMEM((total, HEAD_DIM), BF16),
            pltpu.VMEM((total, HEAD_DIM), BF16),
            pltpu.VMEM((HEAD_DIM, total), BF16),
            pltpu.VMEM((total, HEAD_DIM), BF16),
            pltpu.VMEM((2, total, rows), F32),
            pltpu.VMEM((2, 8, rows), F32),
            pltpu.VMEM((8, rows), F32),
            pltpu.VMEM((HEAD_DIM, rows), F32),
            pltpu.SemaphoreType.DMA((blocks, 3)),
        ],
        compiler_params=pltpu.CompilerParams(vmem_limit_bytes=48 << 20),
        cost_estimate=pl.CostEstimate(
            flops=8 * pairs * HEAD_DIM, bytes_accessed=8 * total * HEAD_DIM, transcendentals=pairs
        ),
        name="flash",
    )(place, *sources)


def join_kernel(place_ref, *refs, blocks, heads):
    parts, out_ref = refs[: blocks * heads], refs[blocks * heads]
    sems = refs[blocks * heads + 1]
    place = place_ref[0]
    copies = []
    for r in range(blocks):
        for h in range(heads):
            column = pl.multiple_of(((place ^ r) * heads + h) * HEAD_DIM, HEAD_DIM)
            copies.append(
                pltpu.make_async_copy(
                    parts[r * heads + h], out_ref.at[:, pl.ds(column, HEAD_DIM)], sems.at[r, h]
                )
            )
            copies[-1].start()
    for copy in copies:
        copy.wait()


def exchange_body(
    gate_inner,
    gate_outer,
    hyena_value,
    decay_rate,
    residue,
    skip_gain,
    filter_index,
    query_rows,
    key_rows,
    value_rows,
    mesh,
):
    ctx_size, tp_size = mesh.shape["ctx"], mesh.shape["tp"]
    row_count, width_cols = query_rows.shape
    heads = width_cols // HEAD_DIM // ctx_size
    place = lax.axis_index("ctx")
    where = place.astype(jnp.int32).reshape(1)
    tiles = gate_inner.shape[1] // LANES

    def swap(a, r):
        return lax.ppermute(a, "ctx", [(i, i ^ r) for i in range(ctx_size)])

    order = sorted(range(1, ctx_size), key=lambda r: (-bin(r >> 1).count("1"), r)) + [0]
    span = math.isqrt(ctx_size - 1) + (math.isqrt(ctx_size - 1) ** 2 < ctx_size - 1)
    got, backs = [], []
    sent = query_rows
    for h in range(heads):
        if h == 1:
            rate, local_residue = gathered_modes(
                decay_rate, residue, filter_index, tiles, tp_size, sent
            )
            part, state = local_part(
                gate_inner, gate_outer, hyena_value, rate, local_residue, skip_gain
            )
            near = [shifted(state, k, ctx_size) for k in range(1, span + 1)]
            sent = state
        packed = pack(where, (after(query_rows, sent), key_rows, value_rows), order, heads, h)
        sent = packed[0]
        mine = [None] * ctx_size
        for piece, r in zip(packed, order):
            mine[r] = swap(piece, r) if r else piece
        got.append(mine)
    for h in range(heads):
        results = flash(where, got[h])
        if h == 0:
            near = lax.optimization_barrier(tuple(near) + (results[0],))[:-1]
            incoming = scan_join(near[0].astype(F32), near[1:], 1, rate, row_count)
            far = [
                shifted(incoming, span * k, ctx_size)
                for k in range(1, span + 1)
                if span * k < ctx_size
            ]
        backs.append([swap(a, r) if r else a for r, a in enumerate(results)])
    far = lax.optimization_barrier(tuple(far) + (results[0],))[:-1]
    incoming = scan_join(incoming, far, span, rate, row_count).astype(BF16)
    hyena_output = remote_part(part, gate_outer, rate, local_residue, incoming)
    parts = [backs[h][r] for r in range(ctx_size) for h in range(heads)]
    parts[0] = after(parts[0], hyena_output)
    attention_output = pl.pallas_call(
        functools.partial(join_kernel, blocks=ctx_size, heads=heads),
        in_specs=[pl.BlockSpec(memory_space=pltpu.SMEM)]
        + [pl.BlockSpec(memory_space=pltpu.VMEM)] * len(parts),
        out_specs=pl.BlockSpec(memory_space=pl.ANY),
        out_shape=jax.ShapeDtypeStruct((row_count, width_cols), BF16),
        scratch_shapes=[pltpu.SemaphoreType.DMA((ctx_size, heads))],
        name="join",
    )(where, *parts)
    return (hyena_output, attention_output)


def row_steps(folded, members, handler, span_rows):
    total_rows = members[0].shape[0]
    block_count = total_rows // span_rows
    stacked = tuple(
        (member.reshape((block_count, span_rows) + member.shape[1:]) for member in members)
    )

    def advance(running, element):
        position, pieces = element
        return (handler(running, pieces, position * span_rows), None)

    folded, _ = lax.scan(advance, folded, (jnp.arange(block_count, dtype=jnp.int32), stacked))
    return folded


def gather_attention(query_rows, key_rows, value_rows):
    row_count, width_cols = query_rows.shape
    head_count = width_cols // HEAD_DIM
    queries = query_rows.reshape(row_count, head_count, HEAD_DIM)
    score_scale = 1.0 / math.sqrt(HEAD_DIM)
    own_rows = lax.axis_index("ctx") * row_count + jnp.arange(row_count, dtype=jnp.int32)

    def attend(folded, pieces, first_row):
        running_max, running_total, summed = folded
        block_rows = pieces[0].shape[0]
        keys_now = pieces[0].reshape(block_rows, head_count, HEAD_DIM)
        values_now = pieces[1].reshape(block_rows, head_count, HEAD_DIM)
        scores = (
            jnp.einsum("thd,shd->hts", queries, keys_now, preferred_element_type=jnp.float32)
            * score_scale
        )
        key_positions = first_row + jnp.arange(block_rows, dtype=jnp.int32)
        visible = own_rows[:, None] >= key_positions[None, :]
        masked = jnp.where(visible[None], scores, floor_score)
        newest = jnp.maximum(running_max, jnp.max(masked, axis=2))
        weights = jnp.where(visible[None], jnp.exp(scores - newest[:, :, None]), 0.0)
        factor = jnp.exp(running_max - newest)
        running_total = running_total * factor + jnp.sum(weights, axis=2)
        update = jnp.einsum(
            "hts,shd->thd",
            weights.astype(jnp.bfloat16),
            values_now,
            preferred_element_type=jnp.float32,
        )
        summed = summed * factor.T[:, :, None] + update
        return (newest, running_total, summed)

    initial = (
        jnp.full((head_count, row_count), floor_score, jnp.float32),
        jnp.zeros((head_count, row_count), jnp.float32),
        jnp.zeros((row_count, head_count, HEAD_DIM), jnp.float32),
    )
    _, running_total, summed = row_steps(
        initial,
        (
            lax.all_gather(key_rows, "ctx", axis=0, tiled=True),
            lax.all_gather(value_rows, "ctx", axis=0, tiled=True),
        ),
        attend,
        512,
    )
    result = summed / running_total.T[:, :, None]
    return result.reshape(row_count, width_cols).astype(jnp.bfloat16)


def solution(mesh):
    ctx_size, tp_size = mesh.shape["ctx"], mesh.shape["tp"]

    def body(
        gate_inner,
        gate_outer,
        hyena_value,
        decay_rate,
        residue,
        skip_gain,
        filter_index,
        query_rows,
        key_rows,
        value_rows,
    ):
        head_count = query_rows.shape[1] // HEAD_DIM
        if head_count % ctx_size == 0 and ctx_size & (ctx_size - 1) == 0 and ctx_size > 2:
            return exchange_body(
                gate_inner,
                gate_outer,
                hyena_value,
                decay_rate,
                residue,
                skip_gain,
                filter_index,
                query_rows,
                key_rows,
                value_rows,
                mesh,
            )
        attention_output = gather_attention(query_rows, key_rows, value_rows)
        tiles = gate_inner.shape[1] // LANES
        modes = gathered_modes(decay_rate, residue, filter_index, tiles, tp_size, None)
        hyena_output = hyena_plain(gate_inner, gate_outer, hyena_value, modes, skip_gain, ctx_size)
        return (hyena_output, attention_output)

    in_specs = (
        P("ctx", "tp"),
        P("ctx", "tp"),
        P("ctx", "tp"),
        P("tp", None),
        P("tp", None),
        P("tp"),
        P("tp"),
        P("ctx", "tp"),
        P("ctx", "tp"),
        P("ctx", "tp"),
    )
    out_specs = (P("ctx", "tp"), P("ctx", "tp"))
    return jax.shard_map(body, mesh=mesh, in_specs=in_specs, out_specs=out_specs, check_vma=False)
```

```python
import functools
import math

import jax
import jax.numpy as jnp
from jax import lax
from jax.experimental import pallas as pl
from jax.experimental.pallas import tpu as pltpu
from jax.sharding import PartitionSpec as P

HEAD_DIM = 128
GROUP = 16
LANES = 128
CHUNK = 128
TILE_GROUPS = LANES // GROUP
STEP_TILES = 4
SPAN = 4

floor_score = -1e30
LOG2E = 1.4426950408889634


F32 = jnp.float32
BF16 = jnp.bfloat16
LAST = (((1,), (1,)), ((), ()))
FIRST = (((0,), (0,)), ((), ()))
PLAIN = (((1,), (0,)), ((), ()))


def mxu(a, b, dims):
    return lax.dot_general(a, b, dims, preferred_element_type=F32)


def halves(a):
    high = a.astype(BF16)
    return high, (a - high.astype(F32)).astype(BF16)


def iota(shape, axis):
    return lax.broadcasted_iota(jnp.int32, shape, axis)


def same_group():
    rows, cols = iota((LANES, LANES), 0), iota((LANES, LANES), 1)
    return (rows // GROUP) == (cols // GROUP)


def carried_pieces(gate_ref, value_ref, lanes):
    rows = gate_ref.shape[0]
    carried = (gate_ref[:, lanes].astype(F32) * value_ref[:, lanes].astype(F32)).astype(BF16)
    return [carried[b * CHUNK : (b + 1) * CHUNK] for b in range(rows // CHUNK)]


def chunk_states(pieces, rate, step, mask):
    ends = jnp.concatenate(halves(jnp.exp((step - CHUNK) * rate)), axis=1)
    full = mxu(jnp.concatenate(pieces, axis=1), ends, FIRST)
    full = full[:, :LANES] + full[:, LANES:]
    return [
        jnp.where(mask, full[b * LANES : (b + 1) * LANES], 0.0) for b in range(len(pieces))
    ]


def spread_states(states, shrinking):
    state_high, state_low = halves(jnp.concatenate(states, axis=0))
    return mxu(
        jnp.concatenate(shrinking, axis=1),
        jnp.concatenate([state_high, state_high], axis=1),
        LAST,
    ) + mxu(shrinking[0], state_low, LAST)


def local_kernel(gate_ref, outer_ref, value_ref, rate_ref, residue_ref, skip_ref, out_ref, state_ref):
    cols = gate_ref.shape[1]
    step = iota((CHUNK, LANES), 0).astype(F32)
    lane_group = iota((CHUNK, LANES), 1) // GROUP
    zero = jnp.zeros((), BF16)
    shape = (CHUNK, TILE_GROUPS * CHUNK)
    causal = iota(shape, 0) >= iota(shape, 1) % CHUNK
    mask = same_group()
    pick = (iota((GROUP, LANES), 1) % GROUP == iota((GROUP, LANES), 0)).astype(BF16)

    def spread(a):
        return jnp.concatenate(
            [jnp.where(lane_group == g, a, zero) for g in range(TILE_GROUPS)], axis=0
        )

    for w in range(cols // LANES):
        lanes = slice(w * LANES, (w + 1) * LANES)
        rate, residue, skip = rate_ref[w], residue_ref[w], skip_ref[w]
        grown_high, grown_low = halves(jnp.exp((step - CHUNK // 2) * rate))
        shrunk = halves(residue * jnp.exp((CHUNK // 2 - step) * rate))
        from_start = halves(residue * jnp.exp(-step * rate))
        decay = jnp.exp(-CHUNK * rate)
        spread_high = spread(grown_high)
        taps = mxu(
            jnp.concatenate(shrunk, axis=1),
            jnp.concatenate([spread_high, spread_high], axis=1),
            LAST,
        ) + mxu(shrunk[0], spread(grown_low), LAST)
        toeplitz = jnp.where(causal, taps, 0.0).astype(BF16)
        pieces = carried_pieces(gate_ref, value_ref, lanes)
        blocks = jnp.concatenate(
            [
                jnp.concatenate(
                    [jnp.where(lane_group == g, piece, zero) for piece in pieces], axis=1
                )
                for g in range(TILE_GROUPS)
            ],
            axis=0,
        )
        inside = mxu(toeplitz, blocks, PLAIN)
        fresh = chunk_states(pieces, rate, step, mask)
        states = [fresh[0]]
        for more in fresh[1:]:
            states.append(states[-1] * decay + more)
        state_ref[w] = mxu(pick, states[-1].astype(BF16), PLAIN).astype(BF16)
        earlier = spread_states(states[:-1], from_start) if len(pieces) > 1 else None
        for b, piece in enumerate(pieces):
            convolved = inside[:, b * LANES : (b + 1) * LANES] + skip * piece.astype(F32)
            if b:
                convolved += earlier[:, (b - 1) * LANES : b * LANES]
            gate = outer_ref[b * CHUNK : (b + 1) * CHUNK, lanes].astype(F32)
            out_ref[b * CHUNK : (b + 1) * CHUNK, lanes] = gate * convolved


def gather_kernel(place_ref, rate_ref, *refs):
    nears, (before_ref, total_ref) = refs[:SPAN], refs[SPAN:]
    spot = place_ref[0] % SPAN
    rows = place_ref[1].astype(F32)
    rate = rate_ref[...]
    before = jnp.zeros(before_ref.shape, F32)
    total = jnp.zeros(before_ref.shape, F32)
    for r, near in enumerate(nears):
        value = near[...].astype(F32)
        j = spot ^ r
        ahead = jnp.maximum(spot - 1 - j, 0).astype(F32) * rows
        faded = value * jnp.exp(-rate * ahead)
        before += jnp.where(j < spot, faded, 0.0)
        total += value * jnp.exp(-rate * ((SPAN - 1 - j).astype(F32) * rows))
    before_ref[...] = before
    total_ref[...] = total.astype(BF16)


def gather_states(where, rate, nears):
    shape = nears[0].shape
    return pl.pallas_call(
        gather_kernel,
        in_specs=[pl.BlockSpec(memory_space=pltpu.SMEM)]
        + [pl.BlockSpec(memory_space=pltpu.VMEM)] * (1 + SPAN),
        out_specs=[pl.BlockSpec(memory_space=pltpu.VMEM)] * 2,
        out_shape=[jax.ShapeDtypeStruct(shape, F32), jax.ShapeDtypeStruct(shape, BF16)],
        name="gather_states",
    )(where, rate, *nears)


def remote_kernel(
    place_ref, part_ref, outer_ref, rate_ref, residue_ref, before_ref, other_ref, out_ref
):
    rows, cols = outer_ref.shape
    step = iota((rows, LANES), 0).astype(F32)
    mask = same_group()
    pick = (iota((LANES, GROUP), 0) % GROUP == iota((LANES, GROUP), 1)).astype(BF16)
    spot = (place_ref[0] % SPAN).astype(F32) * rows
    upper = place_ref[0] >= SPAN
    for w in range(cols // LANES):
        lanes = slice(w * LANES, (w + 1) * LANES)
        rate = rate_ref[w]
        faded = other_ref[w].astype(F32) * jnp.exp(-rate * spot)
        incoming = (before_ref[w] + jnp.where(upper, faded, 0.0)).astype(BF16)
        state = jnp.where(mask, mxu(pick, incoming, PLAIN), 0.0).astype(BF16)
        shrinking = halves(residue_ref[w] * jnp.exp(-step * rate))
        earlier = mxu(
            jnp.concatenate(shrinking, axis=1), jnp.concatenate([state, state], axis=1), LAST
        )
        gate = outer_ref[:, lanes].astype(F32)
        out_ref[:, lanes] = (part_ref[:, lanes] + gate * earlier).astype(BF16)


def after(value, *earlier):
    return lax.optimization_barrier((value,) + earlier)[0]


def gathered_modes(decay_rate, residue, filter_index, tiles, tp_size, gate):
    modes = jnp.concatenate([decay_rate, residue], axis=1)
    if gate is not None:
        modes = after(modes, gate)
    filters, width = modes.shape
    if tp_size <= 4:
        place = lax.axis_index("tp")
        others = [modes] + [
            lax.ppermute(modes, "tp", [(i, (i + shift) % tp_size) for i in range(tp_size)])
            for shift in range(1, tp_size)
        ]
        bank = jnp.concatenate(others, axis=0)
        owner = filter_index // filters
        wanted = (place - owner) % tp_size * filters + filter_index % filters
    else:
        bank = lax.all_gather(modes, "tp", axis=0, tiled=True)
        wanted = filter_index
    chooser = (wanted[:, None] == jnp.arange(bank.shape[0], dtype=jnp.int32)[None, :]).astype(F32)
    local = jnp.dot(chooser, bank, precision=lax.Precision.HIGHEST)
    poles = width // 2
    return (
        local[:, :poles].reshape(tiles, 1, LANES),
        local[:, poles:].reshape(tiles, 1, LANES),
    )


def hyena_specs(row_count, tiles):
    group = math.gcd(tiles, STEP_TILES)
    return (
        (tiles // group,),
        pl.BlockSpec((row_count, group * LANES), lambda i: (0, i)),
        pl.BlockSpec((group, 1, LANES), lambda i: (i, 0, 0)),
        pl.BlockSpec((group, GROUP, LANES), lambda i: (i, 0, 0)),
    )


def local_part(gate_inner, gate_outer, hyena_value, rate, residue, skip_gain):
    row_count, chan_count = gate_inner.shape
    tiles = chan_count // LANES
    grid, wide, row, small = hyena_specs(row_count, tiles)
    return pl.pallas_call(
        local_kernel,
        grid=grid,
        in_specs=[wide, wide, wide, row, row, row],
        out_specs=[wide, small],
        out_shape=[
            jax.ShapeDtypeStruct((row_count, chan_count), F32),
            jax.ShapeDtypeStruct((tiles, GROUP, LANES), BF16),
        ],
        cost_estimate=pl.CostEstimate(
            flops=2 * row_count * chan_count * LANES * 16,
            bytes_accessed=10 * row_count * chan_count,
            transcendentals=row_count * chan_count,
        ),
        name="local_part",
    )(gate_inner, gate_outer, hyena_value, rate, residue, skip_gain.reshape(tiles, 1, LANES))


def remote_part(where, part, gate_outer, rate, residue, before, other):
    row_count, chan_count = gate_outer.shape
    tiles = chan_count // LANES
    grid, wide, row, small = hyena_specs(row_count, tiles)
    return pl.pallas_call(
        remote_kernel,
        grid=grid,
        in_specs=[pl.BlockSpec(memory_space=pltpu.SMEM), wide, wide, row, row, small, small],
        out_specs=wide,
        out_shape=jax.ShapeDtypeStruct((row_count, chan_count), BF16),
        cost_estimate=pl.CostEstimate(
            flops=2 * row_count * chan_count * LANES * 3,
            bytes_accessed=8 * row_count * chan_count,
            transcendentals=row_count * chan_count // 4,
        ),
        name="remote_part",
    )(where, part, gate_outer, rate, residue, before, other)


def shifted(a, by, ctx_size):
    return lax.ppermute(a.astype(BF16), "ctx", [(i, i + by) for i in range(ctx_size - by)])


def scan_join(value, moved, base, rate, rows):
    for k, more in enumerate(moved, 1):
        value = value + more.astype(F32) * jnp.exp(-rate * float(rows * base * k))
    return value


def hyena_plain(gate_inner, gate_outer, hyena_value, modes, skip_gain, ctx_size):
    rate, residue = modes
    rows = gate_inner.shape[0]
    part, state = local_part(gate_inner, gate_outer, hyena_value, rate, residue, skip_gain)
    incoming = shifted(state, 1, ctx_size).astype(F32)
    base = 1
    while base < ctx_size - 1:
        incoming = scan_join(incoming, [shifted(incoming, base, ctx_size)], base, rate, rows)
        base *= 2
    where = jnp.zeros((1,), jnp.int32)
    return remote_part(
        where, part, gate_outer, rate, residue, incoming, jnp.zeros_like(state)
    )


def pack_kernel(place_ref, q_ref, k_ref, v_ref, *refs, spots, heads, head):
    outs, (buf, sems, out_sems) = refs[: len(spots)], refs[len(spots) :]
    place = place_ref[0]
    reads = []
    for n, r in enumerate(spots):
        column = pl.multiple_of(((place ^ r) * heads + head) * HEAD_DIM, HEAD_DIM)
        for j, source in enumerate((q_ref, k_ref, v_ref)):
            reads.append(
                pltpu.make_async_copy(
                    source.at[:, pl.ds(column, HEAD_DIM)],
                    buf.at[n, :, pl.ds(j * HEAD_DIM, HEAD_DIM)],
                    sems.at[n, j],
                )
            )
            reads[-1].start()
    writes = []
    for n in range(len(spots)):
        for j in range(3):
            reads[3 * n + j].wait()
        writes.append(pltpu.make_async_copy(buf.at[n], outs[n], out_sems.at[n]))
        writes[-1].start()
    for write in writes:
        write.wait()


def pack(place, arrays, spots, heads, head):
    rows = arrays[0].shape[0]
    shape = (rows, 3 * HEAD_DIM)
    return pl.pallas_call(
        functools.partial(pack_kernel, spots=spots, heads=heads, head=head),
        in_specs=[pl.BlockSpec(memory_space=pltpu.SMEM)]
        + [pl.BlockSpec(memory_space=pl.ANY)] * 3,
        out_specs=[pl.BlockSpec(memory_space=pl.ANY)] * len(spots),
        out_shape=[jax.ShapeDtypeStruct(shape, BF16)] * len(spots),
        scratch_shapes=[
            pltpu.VMEM((len(spots),) + shape, BF16),
            pltpu.SemaphoreType.DMA((len(spots), 3)),
            pltpu.SemaphoreType.DMA((len(spots),)),
        ],
        cost_estimate=pl.CostEstimate(
            flops=0, bytes_accessed=4 * len(spots) * rows * 3 * HEAD_DIM, transcendentals=0
        ),
        name="pack",
    )(place, *arrays)


def flash_kernel(place_ref, *refs, blocks):
    sources, outs = refs[:blocks], refs[blocks : 2 * blocks]
    q_buf, k_buf, v_buf, vt_buf, o_buf, s_buf, m_buf, l_buf, acc_buf, sems = refs[2 * blocks :]
    rows = sources[0].shape[0]
    place = place_ref[0]
    targets = (q_buf, k_buf, v_buf)

    def fetch(r, block, j):
        spot = pl.ds(pl.multiple_of(block * rows, rows), rows)
        return pltpu.make_async_copy(
            sources[r].at[:, pl.ds(j * HEAD_DIM, HEAD_DIM)], targets[j].at[spot], sems.at[block, j]
        )

    for r in range(blocks):
        for j in range(3):
            fetch(r, place ^ r, j).start()

    def ready(block):
        for j in range(3):
            fetch(0, block, j).wait()
        spot = slice(block * rows, (block + 1) * rows)
        vt_buf[:, spot] = v_buf[spot, :].T

    scale = LOG2E / math.sqrt(HEAD_DIM)

    def score(i, j):
        keys = slice(j * rows, (j + 1) * rows)
        scores = mxu(k_buf[keys, :], q_buf[i * rows : (i + 1) * rows, :], LAST)
        if i == j:
            shape = (rows, rows)
            scores = jnp.where(iota(shape, 1) >= iota(shape, 0), scores, floor_score)
        s_buf[i % 2, keys, :] = scores
        m_buf[i % 2] = jnp.maximum(
            m_buf[i % 2], jnp.max(scores.reshape(rows // 8, 8, rows), axis=0)
        )

    def weigh(i, j, top):
        keys = slice(j * rows, (j + 1) * rows)
        weights = jnp.exp2(s_buf[i % 2, keys, :] * scale - top)
        l_buf[...] += jnp.sum(weights.reshape(rows // 8, 8, rows), axis=0)
        acc_buf[...] += mxu(vt_buf[:, keys], weights.astype(BF16), PLAIN)

    m_buf[...] = jnp.full(m_buf.shape, floor_score, F32)
    ready(0)
    score(0, 0)
    for i in range(blocks):
        if i + 1 < blocks:
            ready(i + 1)
        top = jnp.max(m_buf[i % 2], axis=0, keepdims=True) * scale
        m_buf[(i + 1) % 2] = jnp.full((8, rows), floor_score, F32)
        acc_buf[...] = jnp.zeros(acc_buf.shape, F32)
        l_buf[...] = jnp.zeros(l_buf.shape, F32)
        for j in range(i + 2):
            if j <= i:
                weigh(i, j, top)
            if i + 1 < blocks:
                score(i + 1, j)
        total = jnp.sum(l_buf[...], axis=0, keepdims=True)
        o_buf[i * rows : (i + 1) * rows, :] = (acc_buf[...] / total).T.astype(BF16)
    writes = []
    for r in range(blocks):
        spot = pl.ds(pl.multiple_of((place ^ r) * rows, rows), rows)
        writes.append(pltpu.make_async_copy(o_buf.at[spot], outs[r], sems.at[r, 0]))
        writes[-1].start()
    for write in writes:
        write.wait()


def flash(place, sources):
    blocks, rows = len(sources), sources[0].shape[0]
    total = blocks * rows
    pairs = total * (total + rows) // 2
    return pl.pallas_call(
        functools.partial(flash_kernel, blocks=blocks),
        in_specs=[pl.BlockSpec(memory_space=pltpu.SMEM)]
        + [pl.BlockSpec(memory_space=pl.ANY)] * blocks,
        out_specs=[pl.BlockSpec(memory_space=pl.ANY)] * blocks,
        out_shape=[jax.ShapeDtypeStruct((rows, HEAD_DIM), BF16)] * blocks,
        scratch_shapes=[
            pltpu.VMEM((total, HEAD_DIM), BF16),
            pltpu.VMEM((total, HEAD_DIM), BF16),
            pltpu.VMEM((total, HEAD_DIM), BF16),
            pltpu.VMEM((HEAD_DIM, total), BF16),
            pltpu.VMEM((total, HEAD_DIM), BF16),
            pltpu.VMEM((2, total, rows), F32),
            pltpu.VMEM((2, 8, rows), F32),
            pltpu.VMEM((8, rows), F32),
            pltpu.VMEM((HEAD_DIM, rows), F32),
            pltpu.SemaphoreType.DMA((blocks, 3)),
        ],
        compiler_params=pltpu.CompilerParams(vmem_limit_bytes=48 << 20),
        cost_estimate=pl.CostEstimate(
            flops=8 * pairs * HEAD_DIM, bytes_accessed=8 * total * HEAD_DIM, transcendentals=pairs
        ),
        name="flash",
    )(place, *sources)


def join_kernel(place_ref, *refs, blocks, heads, head):
    parts, out_ref, buf, sems = refs[:blocks], refs[-3], refs[-2], refs[-1]
    place = place_ref[0]
    reads, writes = [], []
    for r in range(blocks):
        reads.append(pltpu.make_async_copy(parts[r], buf.at[r], sems.at[0, r]))
        reads[-1].start()
    for r in range(blocks):
        column = pl.multiple_of(((place ^ r) * heads + head) * HEAD_DIM, HEAD_DIM)
        reads[r].wait()
        writes.append(
            pltpu.make_async_copy(
                buf.at[r], out_ref.at[:, pl.ds(column, HEAD_DIM)], sems.at[1, r]
            )
        )
        writes[-1].start()
    for write in writes:
        write.wait()


def join(place, parts, whole, heads, head):
    blocks = len(parts)
    rows = parts[0].shape[0]
    fresh = whole is None
    operands = tuple(parts) + (() if fresh else (whole,))
    return pl.pallas_call(
        functools.partial(join_kernel, blocks=blocks, heads=heads, head=head),
        in_specs=[pl.BlockSpec(memory_space=pltpu.SMEM)]
        + [pl.BlockSpec(memory_space=pl.ANY)] * len(operands),
        out_specs=pl.BlockSpec(memory_space=pl.ANY),
        out_shape=jax.ShapeDtypeStruct((rows, blocks * heads * HEAD_DIM), BF16),
        scratch_shapes=[
            pltpu.VMEM((blocks, rows, HEAD_DIM), BF16),
            pltpu.SemaphoreType.DMA((2, blocks)),
        ],
        input_output_aliases={} if fresh else {len(operands): 0},
        cost_estimate=pl.CostEstimate(
            flops=0, bytes_accessed=4 * blocks * rows * HEAD_DIM, transcendentals=0
        ),
        name="join",
    )(place, *operands)


def exchange_body(
    gate_inner,
    gate_outer,
    hyena_value,
    decay_rate,
    residue,
    skip_gain,
    filter_index,
    query_rows,
    key_rows,
    value_rows,
    mesh,
):
    ctx_size, tp_size = mesh.shape["ctx"], mesh.shape["tp"]
    row_count, width_cols = query_rows.shape
    heads = width_cols // HEAD_DIM // ctx_size
    place = lax.axis_index("ctx")
    where = place.astype(jnp.int32).reshape(1)
    tiles = gate_inner.shape[1] // LANES

    def swap(a, r):
        return lax.ppermute(a, "ctx", [(i, i ^ r) for i in range(ctx_size)])

    order = sorted(range(1, ctx_size), key=lambda r: (-bin(r >> 1).count("1"), r)) + [0]
    got, backs = [], []
    sent = query_rows
    for h in range(heads):
        packed = pack(where, (after(query_rows, sent), key_rows, value_rows), order, heads, h)
        sent = packed[0]
        if h == 0:
            rate, local_residue = gathered_modes(
                decay_rate, residue, filter_index, tiles, tp_size, sent
            )
        mine = [None] * ctx_size
        for piece, r in zip(packed, order):
            mine[r] = swap(piece, r) if r else piece
        got.append(mine)
    part, state = local_part(gate_inner, gate_outer, hyena_value, rate, local_residue, skip_gain)
    near = [state] + [swap(state, r) for r in range(1, SPAN)]

    for h in range(heads):
        if h == heads - 1:
            near = lax.optimization_barrier(tuple(near) + (backs[-1][0],))[:-1]
            before, total = gather_states(
                jnp.stack([place.astype(jnp.int32), jnp.int32(row_count)]), rate, near
            )
            other = swap(total, SPAN)
        results = flash(where, got[h])
        backs.append([swap(a, r) if r else a for r, a in enumerate(results)])
    before = after(before, backs[-1][0])
    hyena_output = remote_part(where, part, gate_outer, rate, local_residue, before, other)
    attention_output = None
    for h in range(heads):
        attention_output = join(where, backs[h], attention_output, heads, h)
        if h == heads - 2:
            hyena_output, attention_output = lax.optimization_barrier(
                (hyena_output, attention_output)
            )
    return (hyena_output, attention_output)


def row_steps(folded, members, handler, span_rows):
    total_rows = members[0].shape[0]
    block_count = total_rows // span_rows
    stacked = tuple(
        (member.reshape((block_count, span_rows) + member.shape[1:]) for member in members)
    )

    def advance(running, element):
        position, pieces = element
        return (handler(running, pieces, position * span_rows), None)

    folded, _ = lax.scan(advance, folded, (jnp.arange(block_count, dtype=jnp.int32), stacked))
    return folded


def gather_attention(query_rows, key_rows, value_rows):
    row_count, width_cols = query_rows.shape
    head_count = width_cols // HEAD_DIM
    queries = query_rows.reshape(row_count, head_count, HEAD_DIM)
    score_scale = 1.0 / math.sqrt(HEAD_DIM)
    own_rows = lax.axis_index("ctx") * row_count + jnp.arange(row_count, dtype=jnp.int32)

    def attend(folded, pieces, first_row):
        running_max, running_total, summed = folded
        block_rows = pieces[0].shape[0]
        keys_now = pieces[0].reshape(block_rows, head_count, HEAD_DIM)
        values_now = pieces[1].reshape(block_rows, head_count, HEAD_DIM)
        scores = (
            jnp.einsum("thd,shd->hts", queries, keys_now, preferred_element_type=jnp.float32)
            * score_scale
        )
        key_positions = first_row + jnp.arange(block_rows, dtype=jnp.int32)
        visible = own_rows[:, None] >= key_positions[None, :]
        masked = jnp.where(visible[None], scores, floor_score)
        newest = jnp.maximum(running_max, jnp.max(masked, axis=2))
        weights = jnp.where(visible[None], jnp.exp(scores - newest[:, :, None]), 0.0)
        factor = jnp.exp(running_max - newest)
        running_total = running_total * factor + jnp.sum(weights, axis=2)
        update = jnp.einsum(
            "hts,shd->thd",
            weights.astype(jnp.bfloat16),
            values_now,
            preferred_element_type=jnp.float32,
        )
        summed = summed * factor.T[:, :, None] + update
        return (newest, running_total, summed)

    initial = (
        jnp.full((head_count, row_count), floor_score, jnp.float32),
        jnp.zeros((head_count, row_count), jnp.float32),
        jnp.zeros((row_count, head_count, HEAD_DIM), jnp.float32),
    )
    _, running_total, summed = row_steps(
        initial,
        (
            lax.all_gather(key_rows, "ctx", axis=0, tiled=True),
            lax.all_gather(value_rows, "ctx", axis=0, tiled=True),
        ),
        attend,
        512,
    )
    result = summed / running_total.T[:, :, None]
    return result.reshape(row_count, width_cols).astype(jnp.bfloat16)


def solution(mesh):
    ctx_size, tp_size = mesh.shape["ctx"], mesh.shape["tp"]

    def body(
        gate_inner,
        gate_outer,
        hyena_value,
        decay_rate,
        residue,
        skip_gain,
        filter_index,
        query_rows,
        key_rows,
        value_rows,
    ):
        head_count = query_rows.shape[1] // HEAD_DIM
        if head_count % (2 * ctx_size) == 0 and ctx_size == 2 * SPAN:
            return exchange_body(
                gate_inner,
                gate_outer,
                hyena_value,
                decay_rate,
                residue,
                skip_gain,
                filter_index,
                query_rows,
                key_rows,
                value_rows,
                mesh,
            )
        attention_output = gather_attention(query_rows, key_rows, value_rows)
        tiles = gate_inner.shape[1] // LANES
        modes = gathered_modes(decay_rate, residue, filter_index, tiles, tp_size, None)
        hyena_output = hyena_plain(gate_inner, gate_outer, hyena_value, modes, skip_gain, ctx_size)
        return (hyena_output, attention_output)

    in_specs = (
        P("ctx", "tp"),
        P("ctx", "tp"),
        P("ctx", "tp"),
        P("tp", None),
        P("tp", None),
        P("tp"),
        P("tp"),
        P("ctx", "tp"),
        P("ctx", "tp"),
        P("ctx", "tp"),
    )
    out_specs = (P("ctx", "tp"), P("ctx", "tp"))
    return jax.shard_map(body, mesh=mesh, in_specs=in_specs, out_specs=out_specs, check_vma=False)
```

```python
import functools
import math

import jax
import jax.numpy as jnp
from jax import lax
from jax.experimental import pallas as pl
from jax.experimental.pallas import tpu as pltpu
from jax.sharding import PartitionSpec as P

HEAD_DIM = 128
GROUP = 16
LANES = 128
CHUNK = 128
TILE_GROUPS = LANES // GROUP
STEP_TILES = 4
SPAN = 4
SENDS = (6, 7, 4, 2, 5, 3, 1)
WHOLE_VMEM = pltpu.CompilerParams(vmem_limit_bytes=63 << 20)

floor_score = -1e30
LOG2E = 1.4426950408889634


F32 = jnp.float32
BF16 = jnp.bfloat16
LAST = (((1,), (1,)), ((), ()))
FIRST = (((0,), (0,)), ((), ()))
PLAIN = (((1,), (0,)), ((), ()))


def mxu(a, b, dims):
    return lax.dot_general(a, b, dims, preferred_element_type=F32)


def halves(a):
    high = a.astype(BF16)
    return high, (a - high.astype(F32)).astype(BF16)


def iota(shape, axis):
    return lax.broadcasted_iota(jnp.int32, shape, axis)


def same_group():
    rows, cols = iota((LANES, LANES), 0), iota((LANES, LANES), 1)
    return (rows // GROUP) == (cols // GROUP)


def carried_pieces(gate_ref, value_ref, lanes):
    rows = gate_ref.shape[0]
    carried = (gate_ref[:, lanes].astype(F32) * value_ref[:, lanes].astype(F32)).astype(BF16)
    return [carried[b * CHUNK : (b + 1) * CHUNK] for b in range(rows // CHUNK)]


def chunk_states(pieces, rate, step, mask):
    ends = jnp.concatenate(halves(jnp.exp((step - CHUNK) * rate)), axis=1)
    full = mxu(jnp.concatenate(pieces, axis=1), ends, FIRST)
    full = full[:, :LANES] + full[:, LANES:]
    return [
        jnp.where(mask, full[b * LANES : (b + 1) * LANES], 0.0) for b in range(len(pieces))
    ]


def spread_states(states, shrinking):
    state_high, state_low = halves(jnp.concatenate(states, axis=0))
    return mxu(
        jnp.concatenate(shrinking, axis=1),
        jnp.concatenate([state_high, state_high], axis=1),
        LAST,
    ) + mxu(shrinking[0], state_low, LAST)


def local_kernel(gate_ref, outer_ref, value_ref, rate_ref, residue_ref, skip_ref, out_ref, state_ref):
    cols = gate_ref.shape[1]
    step = iota((CHUNK, LANES), 0).astype(F32)
    lane_group = iota((CHUNK, LANES), 1) // GROUP
    zero = jnp.zeros((), BF16)
    shape = (CHUNK, TILE_GROUPS * CHUNK)
    causal = iota(shape, 0) >= iota(shape, 1) % CHUNK
    mask = same_group()
    pick = (iota((GROUP, LANES), 1) % GROUP == iota((GROUP, LANES), 0)).astype(BF16)

    def spread(a):
        return jnp.concatenate(
            [jnp.where(lane_group == g, a, zero) for g in range(TILE_GROUPS)], axis=0
        )

    for w in range(cols // LANES):
        lanes = slice(w * LANES, (w + 1) * LANES)
        rate, residue, skip = rate_ref[w], residue_ref[w], skip_ref[w]
        grown_high, grown_low = halves(jnp.exp((step - CHUNK // 2) * rate))
        shrunk = halves(residue * jnp.exp((CHUNK // 2 - step) * rate))
        from_start = halves(residue * jnp.exp(-step * rate))
        decay = jnp.exp(-CHUNK * rate)
        spread_high = spread(grown_high)
        taps = mxu(
            jnp.concatenate(shrunk, axis=1),
            jnp.concatenate([spread_high, spread_high], axis=1),
            LAST,
        ) + mxu(shrunk[0], spread(grown_low), LAST)
        toeplitz = jnp.where(causal, taps, 0.0).astype(BF16)
        pieces = carried_pieces(gate_ref, value_ref, lanes)
        blocks = jnp.concatenate(
            [
                jnp.concatenate(
                    [jnp.where(lane_group == g, piece, zero) for piece in pieces], axis=1
                )
                for g in range(TILE_GROUPS)
            ],
            axis=0,
        )
        inside = mxu(toeplitz, blocks, PLAIN)
        fresh = chunk_states(pieces, rate, step, mask)
        states = [fresh[0]]
        for more in fresh[1:]:
            states.append(states[-1] * decay + more)
        state_ref[w] = mxu(pick, states[-1].astype(BF16), PLAIN).astype(BF16)
        earlier = spread_states(states[:-1], from_start) if len(pieces) > 1 else None
        for b, piece in enumerate(pieces):
            convolved = inside[:, b * LANES : (b + 1) * LANES] + skip * piece.astype(F32)
            if b:
                convolved += earlier[:, (b - 1) * LANES : b * LANES]
            gate = outer_ref[b * CHUNK : (b + 1) * CHUNK, lanes].astype(F32)
            out_ref[b * CHUNK : (b + 1) * CHUNK, lanes] = gate * convolved


def gather_kernel(place_ref, rate_ref, *refs):
    nears, (before_ref, total_ref) = refs[:SPAN], refs[SPAN:]
    spot = place_ref[0] % SPAN
    rows = place_ref[1].astype(F32)
    rate = rate_ref[...]
    before = jnp.zeros(before_ref.shape, F32)
    total = jnp.zeros(before_ref.shape, F32)
    for r, near in enumerate(nears):
        value = near[...].astype(F32)
        j = spot ^ r
        ahead = jnp.maximum(spot - 1 - j, 0).astype(F32) * rows
        faded = value * jnp.exp(-rate * ahead)
        before += jnp.where(j < spot, faded, 0.0)
        total += value * jnp.exp(-rate * ((SPAN - 1 - j).astype(F32) * rows))
    before_ref[...] = before
    total_ref[...] = total.astype(BF16)


def gather_states(where, rate, nears):
    shape = nears[0].shape
    return pl.pallas_call(
        gather_kernel,
        in_specs=[pl.BlockSpec(memory_space=pltpu.SMEM)]
        + [pl.BlockSpec(memory_space=pltpu.VMEM)] * (1 + SPAN),
        out_specs=[pl.BlockSpec(memory_space=pltpu.VMEM)] * 2,
        out_shape=[jax.ShapeDtypeStruct(shape, F32), jax.ShapeDtypeStruct(shape, BF16)],
        compiler_params=WHOLE_VMEM,
        name="gather_states",
    )(where, rate, *nears)


def remote_kernel(
    place_ref, part_ref, outer_ref, rate_ref, residue_ref, before_ref, other_ref, out_ref
):
    rows, cols = outer_ref.shape
    step = iota((CHUNK, LANES), 0).astype(F32)
    mask = same_group()
    pick = (iota((LANES, GROUP), 0) % GROUP == iota((LANES, GROUP), 1)).astype(BF16)
    spot = (place_ref[0] % SPAN).astype(F32) * rows
    upper = place_ref[0] >= SPAN
    for w in range(cols // LANES):
        lanes = slice(w * LANES, (w + 1) * LANES)
        rate = rate_ref[w]
        faded = other_ref[w].astype(F32) * jnp.exp(-rate * spot)
        incoming = (before_ref[w] + jnp.where(upper, faded, 0.0)).astype(BF16)
        state = jnp.where(mask, mxu(pick, incoming, PLAIN), 0.0).astype(BF16)
        decay = jnp.exp(-CHUNK * rate)
        shrinking = [residue_ref[w] * jnp.exp(-step * rate)]
        while len(shrinking) < rows // CHUNK:
            shrinking.append(shrinking[-1] * decay)
        earlier = mxu(jnp.concatenate(shrinking, axis=0).astype(BF16), state, LAST)
        gate = outer_ref[:, lanes].astype(F32)
        out_ref[:, lanes] = (part_ref[:, lanes] + gate * earlier).astype(BF16)


def after(value, *earlier):
    return lax.optimization_barrier((value,) + earlier)[0]


def gathered_modes(decay_rate, residue, filter_index, tiles, tp_size, gate):
    modes = jnp.concatenate([decay_rate, residue], axis=1)
    if gate is not None:
        modes = after(modes, gate)
    filters, width = modes.shape
    if tp_size <= 4:
        place = lax.axis_index("tp")
        others = [modes] + [
            lax.ppermute(modes, "tp", [(i, (i + shift) % tp_size) for i in range(tp_size)])
            for shift in range(1, tp_size)
        ]
        bank = jnp.concatenate(others, axis=0)
        owner = filter_index // filters
        wanted = (place - owner) % tp_size * filters + filter_index % filters
    else:
        bank = lax.all_gather(modes, "tp", axis=0, tiled=True)
        wanted = filter_index
    chooser = (wanted[:, None] == jnp.arange(bank.shape[0], dtype=jnp.int32)[None, :]).astype(F32)
    local = jnp.dot(chooser, bank, precision=lax.Precision.HIGHEST)
    poles = width // 2
    return (
        local[:, :poles].reshape(tiles, 1, LANES),
        local[:, poles:].reshape(tiles, 1, LANES),
    )


def hyena_specs(row_count, tiles, most=STEP_TILES):
    group = math.gcd(tiles, most)
    return (
        (tiles // group,),
        pl.BlockSpec((row_count, group * LANES), lambda i: (0, i)),
        pl.BlockSpec((group, 1, LANES), lambda i: (i, 0, 0)),
        pl.BlockSpec((group, GROUP, LANES), lambda i: (i, 0, 0)),
    )


def local_part(gate_inner, gate_outer, hyena_value, rate, residue, skip_gain):
    row_count, chan_count = gate_inner.shape
    tiles = chan_count // LANES
    grid, wide, row, small = hyena_specs(row_count, tiles)
    return pl.pallas_call(
        local_kernel,
        grid=grid,
        in_specs=[wide, wide, wide, row, row, row],
        out_specs=[wide, small],
        out_shape=[
            jax.ShapeDtypeStruct((row_count, chan_count), F32),
            jax.ShapeDtypeStruct((tiles, GROUP, LANES), BF16),
        ],
        cost_estimate=pl.CostEstimate(
            flops=2 * row_count * chan_count * LANES * 16,
            bytes_accessed=10 * row_count * chan_count,
            transcendentals=row_count * chan_count,
        ),
        compiler_params=WHOLE_VMEM,
        name="local_part",
    )(gate_inner, gate_outer, hyena_value, rate, residue, skip_gain.reshape(tiles, 1, LANES))


def remote_part(where, part, gate_outer, rate, residue, before, other):
    row_count, chan_count = gate_outer.shape
    tiles = chan_count // LANES
    grid, wide, row, small = hyena_specs(row_count, tiles, 4)
    return pl.pallas_call(
        remote_kernel,
        grid=grid,
        in_specs=[pl.BlockSpec(memory_space=pltpu.SMEM), wide, wide, row, row, small, small],
        out_specs=wide,
        out_shape=jax.ShapeDtypeStruct((row_count, chan_count), BF16),
        cost_estimate=pl.CostEstimate(
            flops=2 * row_count * chan_count * LANES * 3,
            bytes_accessed=8 * row_count * chan_count,
            transcendentals=row_count * chan_count // 4,
        ),
        compiler_params=WHOLE_VMEM,
        name="remote_part",
    )(where, part, gate_outer, rate, residue, before, other)


def shifted(a, by, ctx_size):
    return lax.ppermute(a.astype(BF16), "ctx", [(i, i + by) for i in range(ctx_size - by)])


def scan_join(value, moved, base, rate, rows):
    for k, more in enumerate(moved, 1):
        value = value + more.astype(F32) * jnp.exp(-rate * float(rows * base * k))
    return value


def hyena_plain(gate_inner, gate_outer, hyena_value, modes, skip_gain, ctx_size):
    rate, residue = modes
    rows = gate_inner.shape[0]
    part, state = local_part(gate_inner, gate_outer, hyena_value, rate, residue, skip_gain)
    incoming = shifted(state, 1, ctx_size).astype(F32)
    base = 1
    while base < ctx_size - 1:
        incoming = scan_join(incoming, [shifted(incoming, base, ctx_size)], base, rate, rows)
        base *= 2
    where = jnp.zeros((1,), jnp.int32)
    return remote_part(
        where, part, gate_outer, rate, residue, incoming, jnp.zeros_like(state)
    )


def pack_kernel(place_ref, q_ref, k_ref, v_ref, *refs, spots, heads, head):
    outs, (buf, sems, out_sems) = refs[: len(spots)], refs[len(spots) :]
    place = place_ref[0]
    reads = []
    for n, r in enumerate(spots):
        column = pl.multiple_of(((place ^ r) * heads + head) * HEAD_DIM, HEAD_DIM)
        for j, source in enumerate((q_ref, k_ref, v_ref)):
            reads.append(
                pltpu.make_async_copy(
                    source.at[:, pl.ds(column, HEAD_DIM)],
                    buf.at[n, :, pl.ds(j * HEAD_DIM, HEAD_DIM)],
                    sems.at[n, j],
                )
            )
            reads[-1].start()
    writes = []
    for n in range(len(spots)):
        for j in range(3):
            reads[3 * n + j].wait()
        writes.append(pltpu.make_async_copy(buf.at[n], outs[n], out_sems.at[n]))
        writes[-1].start()
    for write in writes:
        write.wait()


def pack(place, arrays, spots, heads, head):
    rows = arrays[0].shape[0]
    shape = (rows, 3 * HEAD_DIM)
    return pl.pallas_call(
        functools.partial(pack_kernel, spots=spots, heads=heads, head=head),
        in_specs=[pl.BlockSpec(memory_space=pltpu.SMEM)]
        + [pl.BlockSpec(memory_space=pl.ANY)] * 3,
        out_specs=[pl.BlockSpec(memory_space=pl.ANY)] * len(spots),
        out_shape=[jax.ShapeDtypeStruct(shape, BF16)] * len(spots),
        scratch_shapes=[
            pltpu.VMEM((len(spots),) + shape, BF16),
            pltpu.SemaphoreType.DMA((len(spots), 3)),
            pltpu.SemaphoreType.DMA((len(spots),)),
        ],
        cost_estimate=pl.CostEstimate(
            flops=0, bytes_accessed=4 * len(spots) * rows * 3 * HEAD_DIM, transcendentals=0
        ),
        compiler_params=WHOLE_VMEM,
        name="pack",
    )(place, *arrays)


def flash_kernel(place_ref, *refs, blocks):
    sources, outs = refs[:blocks], refs[blocks : 2 * blocks]
    q_buf, k_buf, v_buf, vt_buf, o_buf, s_buf, m_buf, l_buf, acc_buf, sems = refs[2 * blocks :]
    rows = sources[0].shape[0]
    place = place_ref[0]
    targets = (q_buf, k_buf, v_buf)

    def fetch(r, block, j):
        spot = pl.ds(pl.multiple_of(block * rows, rows), rows)
        return pltpu.make_async_copy(
            sources[r].at[:, pl.ds(j * HEAD_DIM, HEAD_DIM)], targets[j].at[spot], sems.at[block, j]
        )

    for r in range(blocks):
        for j in range(3):
            fetch(r, place ^ r, j).start()

    def ready(block):
        for j in range(3):
            fetch(0, block, j).wait()
        spot = slice(block * rows, (block + 1) * rows)
        vt_buf[:, spot] = v_buf[spot, :].T

    scale = LOG2E / math.sqrt(HEAD_DIM)

    half = rows // 2

    def score_part(i, keys, first, masked):
        queries = slice(i * rows + first, (i + 1) * rows)
        scores = mxu(k_buf[keys, :], q_buf[queries, :], LAST)
        shape = scores.shape
        if masked:
            scores = jnp.where(iota(shape, 1) >= iota(shape, 0), scores, floor_score)
        s_buf[i % 2, keys, first:] = scores
        m_buf[i % 2, :, first:] = jnp.maximum(
            m_buf[i % 2, :, first:], jnp.max(scores.reshape(shape[0] // 8, 8, shape[1]), axis=0)
        )

    def weigh_part(i, keys, first, top):
        weights = jnp.exp2(s_buf[i % 2, keys, first:] * scale - top[:, first:])
        shape = weights.shape
        l_buf[:, first:] += jnp.sum(weights.reshape(shape[0] // 8, 8, shape[1]), axis=0)
        acc_buf[:, first:] += mxu(vt_buf[:, keys], weights.astype(BF16), PLAIN)

    def spans(i, j):
        if i != j:
            return [(slice(j * rows, (j + 1) * rows), 0)]
        return [
            (slice(j * rows, j * rows + half), 0),
            (slice(j * rows + half, (j + 1) * rows), half),
        ]

    def score(i, j):
        for keys, first in spans(i, j):
            score_part(i, keys, first, i == j)

    def weigh(i, j, top):
        for keys, first in spans(i, j):
            weigh_part(i, keys, first, top)

    m_buf[...] = jnp.full(m_buf.shape, floor_score, F32)
    ready(0)
    score(0, 0)
    for i in range(blocks):
        if i + 1 < blocks:
            ready(i + 1)
        top = jnp.max(m_buf[i % 2], axis=0, keepdims=True) * scale
        m_buf[(i + 1) % 2] = jnp.full((8, rows), floor_score, F32)
        acc_buf[...] = jnp.zeros(acc_buf.shape, F32)
        l_buf[...] = jnp.zeros(l_buf.shape, F32)
        for j in range(i + 2):
            if j <= i:
                weigh(i, j, top)
            if i + 1 < blocks:
                score(i + 1, j)
        total = jnp.sum(l_buf[...], axis=0, keepdims=True)
        o_buf[i * rows : (i + 1) * rows, :] = (acc_buf[...] / total).T.astype(BF16)
    writes = []
    for r in range(blocks):
        spot = pl.ds(pl.multiple_of((place ^ r) * rows, rows), rows)
        writes.append(pltpu.make_async_copy(o_buf.at[spot], outs[r], sems.at[r, 0]))
        writes[-1].start()
    for write in writes:
        write.wait()


def flash(place, sources):
    blocks, rows = len(sources), sources[0].shape[0]
    total = blocks * rows
    pairs = total * (total + rows) // 2
    return pl.pallas_call(
        functools.partial(flash_kernel, blocks=blocks),
        in_specs=[pl.BlockSpec(memory_space=pltpu.SMEM)]
        + [pl.BlockSpec(memory_space=pl.ANY)] * blocks,
        out_specs=[pl.BlockSpec(memory_space=pl.ANY)] * blocks,
        out_shape=[jax.ShapeDtypeStruct((rows, HEAD_DIM), BF16)] * blocks,
        scratch_shapes=[
            pltpu.VMEM((total, HEAD_DIM), BF16),
            pltpu.VMEM((total, HEAD_DIM), BF16),
            pltpu.VMEM((total, HEAD_DIM), BF16),
            pltpu.VMEM((HEAD_DIM, total), BF16),
            pltpu.VMEM((total, HEAD_DIM), BF16),
            pltpu.VMEM((2, total, rows), F32),
            pltpu.VMEM((2, 8, rows), F32),
            pltpu.VMEM((8, rows), F32),
            pltpu.VMEM((HEAD_DIM, rows), F32),
            pltpu.SemaphoreType.DMA((blocks, 3)),
        ],
        compiler_params=WHOLE_VMEM,
        cost_estimate=pl.CostEstimate(
            flops=8 * pairs * HEAD_DIM, bytes_accessed=8 * total * HEAD_DIM, transcendentals=pairs
        ),
        name="flash",
    )(place, *sources)


def join_kernel(place_ref, *refs, blocks, heads):
    count = blocks * heads
    parts, out_ref, buf, sems = refs[:count], refs[-3], refs[-2], refs[-1]
    place = place_ref[0]
    reads, writes = [], []
    for n in range(count):
        reads.append(pltpu.make_async_copy(parts[n], buf.at[n], sems.at[0, n]))
        reads[-1].start()
    for n in range(count):
        column = pl.multiple_of(((place ^ (n % blocks)) * heads + n // blocks) * HEAD_DIM, HEAD_DIM)
        reads[n].wait()
        writes.append(
            pltpu.make_async_copy(buf.at[n], out_ref.at[:, pl.ds(column, HEAD_DIM)], sems.at[1, n])
        )
        writes[-1].start()
    for write in writes:
        write.wait()


def join(place, backs):
    heads, blocks = len(backs), len(backs[0])
    parts = [a for back in backs for a in back]
    rows = parts[0].shape[0]
    return pl.pallas_call(
        functools.partial(join_kernel, blocks=blocks, heads=heads),
        in_specs=[pl.BlockSpec(memory_space=pltpu.SMEM)]
        + [pl.BlockSpec(memory_space=pl.ANY)] * len(parts),
        out_specs=pl.BlockSpec(memory_space=pl.ANY),
        out_shape=jax.ShapeDtypeStruct((rows, blocks * heads * HEAD_DIM), BF16),
        scratch_shapes=[
            pltpu.VMEM((len(parts), rows, HEAD_DIM), BF16),
            pltpu.SemaphoreType.DMA((2, len(parts))),
        ],
        compiler_params=WHOLE_VMEM,
        cost_estimate=pl.CostEstimate(
            flops=0, bytes_accessed=4 * len(parts) * rows * HEAD_DIM, transcendentals=0
        ),
        name="join",
    )(place, *parts)


def exchange_body(
    gate_inner,
    gate_outer,
    hyena_value,
    decay_rate,
    residue,
    skip_gain,
    filter_index,
    query_rows,
    key_rows,
    value_rows,
    mesh,
):
    ctx_size, tp_size = mesh.shape["ctx"], mesh.shape["tp"]
    row_count, width_cols = query_rows.shape
    heads = width_cols // HEAD_DIM // ctx_size
    place = lax.axis_index("ctx")
    where = place.astype(jnp.int32).reshape(1)
    tiles = gate_inner.shape[1] // LANES

    def swap(a, r):
        return lax.ppermute(a, "ctx", [(i, i ^ r) for i in range(ctx_size)])

    order = list(SENDS) + [0]
    got, backs = [], []
    sent = query_rows
    lead = 2
    for h in range(heads):
        mine = [None] * ctx_size
        pieces = [order[:lead], order[lead:]] if h == 0 else [order]
        for some in pieces:
            packed = pack(where, (after(query_rows, sent), key_rows, value_rows), some, heads, h)
            sent = packed[0]
            for piece, r in zip(packed, some):
                mine[r] = swap(piece, r) if r else piece
        if h == 0:
            rate, local_residue = gathered_modes(
                decay_rate, residue, filter_index, tiles, tp_size, sent
            )
        got.append(mine)
    part, state = local_part(gate_inner, gate_outer, hyena_value, rate, local_residue, skip_gain)
    near = [state] + [swap(state, r) for r in range(1, SPAN)]

    for h in range(heads):
        results = flash(where, got[h])
        if h == heads - 2:
            near = lax.optimization_barrier(tuple(near) + (results[0],))[:-1]
            before, total = gather_states(
                jnp.stack([place.astype(jnp.int32), jnp.int32(row_count)]), rate, near
            )
            other = swap(total, SPAN)
        back = list(results)
        for r in SENDS:
            back[r] = swap(results[r], r)
        backs.append(back)
    before = after(before, backs[-1][0])
    hyena_output = remote_part(where, part, gate_outer, rate, local_residue, before, other)
    backs[-1][0] = after(backs[-1][0], hyena_output)
    return (hyena_output, join(where, backs))


def row_steps(folded, members, handler, span_rows):
    total_rows = members[0].shape[0]
    block_count = total_rows // span_rows
    stacked = tuple(
        (member.reshape((block_count, span_rows) + member.shape[1:]) for member in members)
    )

    def advance(running, element):
        position, pieces = element
        return (handler(running, pieces, position * span_rows), None)

    folded, _ = lax.scan(advance, folded, (jnp.arange(block_count, dtype=jnp.int32), stacked))
    return folded


def gather_attention(query_rows, key_rows, value_rows):
    row_count, width_cols = query_rows.shape
    head_count = width_cols // HEAD_DIM
    queries = query_rows.reshape(row_count, head_count, HEAD_DIM)
    score_scale = 1.0 / math.sqrt(HEAD_DIM)
    own_rows = lax.axis_index("ctx") * row_count + jnp.arange(row_count, dtype=jnp.int32)

    def attend(folded, pieces, first_row):
        running_max, running_total, summed = folded
        block_rows = pieces[0].shape[0]
        keys_now = pieces[0].reshape(block_rows, head_count, HEAD_DIM)
        values_now = pieces[1].reshape(block_rows, head_count, HEAD_DIM)
        scores = (
            jnp.einsum("thd,shd->hts", queries, keys_now, preferred_element_type=jnp.float32)
            * score_scale
        )
        key_positions = first_row + jnp.arange(block_rows, dtype=jnp.int32)
        visible = own_rows[:, None] >= key_positions[None, :]
        masked = jnp.where(visible[None], scores, floor_score)
        newest = jnp.maximum(running_max, jnp.max(masked, axis=2))
        weights = jnp.where(visible[None], jnp.exp(scores - newest[:, :, None]), 0.0)
        factor = jnp.exp(running_max - newest)
        running_total = running_total * factor + jnp.sum(weights, axis=2)
        update = jnp.einsum(
            "hts,shd->thd",
            weights.astype(jnp.bfloat16),
            values_now,
            preferred_element_type=jnp.float32,
        )
        summed = summed * factor.T[:, :, None] + update
        return (newest, running_total, summed)

    initial = (
        jnp.full((head_count, row_count), floor_score, jnp.float32),
        jnp.zeros((head_count, row_count), jnp.float32),
        jnp.zeros((row_count, head_count, HEAD_DIM), jnp.float32),
    )
    _, running_total, summed = row_steps(
        initial,
        (
            lax.all_gather(key_rows, "ctx", axis=0, tiled=True),
            lax.all_gather(value_rows, "ctx", axis=0, tiled=True),
        ),
        attend,
        512,
    )
    result = summed / running_total.T[:, :, None]
    return result.reshape(row_count, width_cols).astype(jnp.bfloat16)


def solution(mesh):
    ctx_size, tp_size = mesh.shape["ctx"], mesh.shape["tp"]

    def body(
        gate_inner,
        gate_outer,
        hyena_value,
        decay_rate,
        residue,
        skip_gain,
        filter_index,
        query_rows,
        key_rows,
        value_rows,
    ):
        head_count = query_rows.shape[1] // HEAD_DIM
        if head_count % (2 * ctx_size) == 0 and ctx_size == 2 * SPAN:
            return exchange_body(
                gate_inner,
                gate_outer,
                hyena_value,
                decay_rate,
                residue,
                skip_gain,
                filter_index,
                query_rows,
                key_rows,
                value_rows,
                mesh,
            )
        attention_output = gather_attention(query_rows, key_rows, value_rows)
        tiles = gate_inner.shape[1] // LANES
        modes = gathered_modes(decay_rate, residue, filter_index, tiles, tp_size, None)
        hyena_output = hyena_plain(gate_inner, gate_outer, hyena_value, modes, skip_gain, ctx_size)
        return (hyena_output, attention_output)

    in_specs = (
        P("ctx", "tp"),
        P("ctx", "tp"),
        P("ctx", "tp"),
        P("tp", None),
        P("tp", None),
        P("tp"),
        P("tp"),
        P("ctx", "tp"),
        P("ctx", "tp"),
        P("ctx", "tp"),
    )
    out_specs = (P("ctx", "tp"), P("ctx", "tp"))
    return jax.shard_map(body, mesh=mesh, in_specs=in_specs, out_specs=out_specs, check_vma=False)
```

```python
import functools
import math

import jax
import jax.numpy as jnp
from jax import lax
from jax.experimental import pallas as pl
from jax.experimental.pallas import tpu as pltpu
from jax.sharding import PartitionSpec as P

HEAD_DIM = 128
GROUP = 16
LANES = 128
CHUNK = 128
TILE_GROUPS = LANES // GROUP
STEP_TILES = 4
SPAN = 4
SENDS = (6, 7, 4, 2, 5, 3, 1)
WHOLE_VMEM = pltpu.CompilerParams(vmem_limit_bytes=63 << 20)

floor_score = -1e30
LOG2E = 1.4426950408889634
TOO_SMALL = 2.0**-80


F32 = jnp.float32
BF16 = jnp.bfloat16
LAST = (((1,), (1,)), ((), ()))
FIRST = (((0,), (0,)), ((), ()))
PLAIN = (((1,), (0,)), ((), ()))


def mxu(a, b, dims):
    return lax.dot_general(a, b, dims, preferred_element_type=F32)


def halves(a):
    high = a.astype(BF16)
    return high, (a - high.astype(F32)).astype(BF16)


def iota(shape, axis):
    return lax.broadcasted_iota(jnp.int32, shape, axis)


def same_group():
    rows, cols = iota((LANES, LANES), 0), iota((LANES, LANES), 1)
    return (rows // GROUP) == (cols // GROUP)


def carried_pieces(gate_ref, value_ref, lanes):
    rows = gate_ref.shape[0]
    carried = (gate_ref[:, lanes].astype(F32) * value_ref[:, lanes].astype(F32)).astype(BF16)
    return [carried[b * CHUNK : (b + 1) * CHUNK] for b in range(rows // CHUNK)]


def chunk_states(pieces, rate, step, mask):
    ends = jnp.concatenate(halves(jnp.exp((step - CHUNK) * rate)), axis=1)
    full = mxu(jnp.concatenate(pieces, axis=1), ends, FIRST)
    full = full[:, :LANES] + full[:, LANES:]
    return [
        jnp.where(mask, full[b * LANES : (b + 1) * LANES], 0.0) for b in range(len(pieces))
    ]


def spread_states(states, shrinking):
    state_high, state_low = halves(jnp.concatenate(states, axis=0))
    return mxu(
        jnp.concatenate(shrinking, axis=1),
        jnp.concatenate([state_high, state_high], axis=1),
        LAST,
    ) + mxu(shrinking[0], state_low, LAST)


def local_kernel(gate_ref, outer_ref, value_ref, rate_ref, residue_ref, skip_ref, out_ref, state_ref):
    cols = gate_ref.shape[1]
    step = iota((CHUNK, LANES), 0).astype(F32)
    lane_group = iota((CHUNK, LANES), 1) // GROUP
    zero = jnp.zeros((), BF16)
    shape = (CHUNK, TILE_GROUPS * CHUNK)
    causal = iota(shape, 0) >= iota(shape, 1) % CHUNK
    mask = same_group()
    pick = (iota((GROUP, LANES), 1) % GROUP == iota((GROUP, LANES), 0)).astype(BF16)

    def spread(a):
        return jnp.concatenate(
            [jnp.where(lane_group == g, a, zero) for g in range(TILE_GROUPS)], axis=0
        )

    for w in range(cols // LANES):
        lanes = slice(w * LANES, (w + 1) * LANES)
        rate, residue, skip = rate_ref[w], residue_ref[w], skip_ref[w]
        grown_high, grown_low = halves(jnp.exp((step - CHUNK // 2) * rate))
        shrunk = halves(residue * jnp.exp((CHUNK // 2 - step) * rate))
        from_start = halves(residue * jnp.exp(-step * rate))
        decay = jnp.exp(-CHUNK * rate)
        spread_high = spread(grown_high)
        taps = mxu(
            jnp.concatenate(shrunk, axis=1),
            jnp.concatenate([spread_high, spread_high], axis=1),
            LAST,
        ) + mxu(shrunk[0], spread(grown_low), LAST)
        toeplitz = jnp.where(causal, taps, 0.0).astype(BF16)
        pieces = carried_pieces(gate_ref, value_ref, lanes)
        blocks = jnp.concatenate(
            [
                jnp.concatenate(
                    [jnp.where(lane_group == g, piece, zero) for piece in pieces], axis=1
                )
                for g in range(TILE_GROUPS)
            ],
            axis=0,
        )
        inside = mxu(toeplitz, blocks, PLAIN)
        fresh = chunk_states(pieces, rate, step, mask)
        states = [fresh[0]]
        for more in fresh[1:]:
            states.append(states[-1] * decay + more)
        state_ref[w] = mxu(pick, states[-1].astype(BF16), PLAIN).astype(BF16)
        earlier = spread_states(states[:-1], from_start) if len(pieces) > 1 else None
        for b, piece in enumerate(pieces):
            convolved = inside[:, b * LANES : (b + 1) * LANES] + skip * piece.astype(F32)
            if b:
                convolved += earlier[:, (b - 1) * LANES : b * LANES]
            gate = outer_ref[b * CHUNK : (b + 1) * CHUNK, lanes].astype(F32)
            out_ref[b * CHUNK : (b + 1) * CHUNK, lanes] = gate * convolved


def pair_kernel(place_ref, rate_ref, mine_ref, other_ref, total_ref):
    mine, other = mine_ref[...].astype(F32), other_ref[...].astype(F32)
    second = place_ref[0] % 2 == 1
    lower, upper = jnp.where(second, other, mine), jnp.where(second, mine, other)
    rows = place_ref[1].astype(F32)
    total_ref[...] = (lower * jnp.exp(-rate_ref[...] * rows) + upper).astype(BF16)


def gather_kernel(place_ref, rate_ref, other_ref, pair_ref, far_ref, before_ref, total_ref):
    core, side = place_ref[0] % 2, (place_ref[0] // 2) % 2
    rows = place_ref[1].astype(F32)
    rate = rate_ref[...]
    pair, far = pair_ref[...].astype(F32), far_ref[...].astype(F32)
    faded = far * jnp.exp(-rate * (core.astype(F32) * rows))
    before_ref[...] = jnp.where(core == 1, other_ref[...].astype(F32), 0.0) + jnp.where(
        side == 1, faded, 0.0
    )
    lower, upper = jnp.where(side == 1, far, pair), jnp.where(side == 1, pair, far)
    total_ref[...] = (lower * jnp.exp(-rate * (2.0 * rows)) + upper).astype(BF16)


def state_call(kernel, where, rate, states, kinds):
    shape = states[0].shape
    return pl.pallas_call(
        kernel,
        in_specs=[pl.BlockSpec(memory_space=pltpu.SMEM)]
        + [pl.BlockSpec(memory_space=pltpu.VMEM)] * (1 + len(states)),
        out_specs=[pl.BlockSpec(memory_space=pltpu.VMEM)] * len(kinds),
        out_shape=[jax.ShapeDtypeStruct(shape, kind) for kind in kinds],
        compiler_params=WHOLE_VMEM,
    )(where, rate, *states)


def remote_kernel(
    place_ref, part_ref, outer_ref, rate_ref, residue_ref, before_ref, other_ref, out_ref
):
    rows, cols = outer_ref.shape
    step = iota((CHUNK, LANES), 0).astype(F32)
    mask = same_group()
    pick = (iota((LANES, GROUP), 0) % GROUP == iota((LANES, GROUP), 1)).astype(BF16)
    spot = (place_ref[0] % SPAN).astype(F32) * rows
    upper = place_ref[0] >= SPAN
    for w in range(cols // LANES):
        lanes = slice(w * LANES, (w + 1) * LANES)
        rate = rate_ref[w]
        faded = other_ref[w].astype(F32) * jnp.exp(-rate * spot)
        incoming = (before_ref[w] + jnp.where(upper, faded, 0.0)).astype(BF16)
        state = jnp.where(mask, mxu(pick, incoming, PLAIN), 0.0).astype(BF16)
        decay = jnp.exp(-CHUNK * rate)
        shrinking = [residue_ref[w] * jnp.exp(-step * rate)]
        while len(shrinking) < rows // CHUNK:
            shrinking.append(shrinking[-1] * decay)
        earlier = mxu(jnp.concatenate(shrinking, axis=0).astype(BF16), state, LAST)
        gate = outer_ref[:, lanes].astype(F32)
        out_ref[:, lanes] = (part_ref[:, lanes] + gate * earlier).astype(BF16)


def after(value, *earlier):
    return lax.optimization_barrier((value,) + earlier)[0]


def gathered_modes(decay_rate, residue, filter_index, tiles, tp_size, gate):
    modes = jnp.concatenate([decay_rate, residue], axis=1)
    if gate is not None:
        modes = after(modes, gate)
    filters, width = modes.shape
    if tp_size <= 4:
        place = lax.axis_index("tp")
        others = [modes] + [
            lax.ppermute(modes, "tp", [(i, (i + shift) % tp_size) for i in range(tp_size)])
            for shift in range(1, tp_size)
        ]
        bank = jnp.concatenate(others, axis=0)
        owner = filter_index // filters
        wanted = (place - owner) % tp_size * filters + filter_index % filters
    else:
        bank = lax.all_gather(modes, "tp", axis=0, tiled=True)
        wanted = filter_index
    chooser = (wanted[:, None] == jnp.arange(bank.shape[0], dtype=jnp.int32)[None, :]).astype(F32)
    local = jnp.dot(chooser, bank, precision=lax.Precision.HIGHEST)
    poles = width // 2
    return (
        local[:, :poles].reshape(tiles, 1, LANES),
        local[:, poles:].reshape(tiles, 1, LANES),
    )


def hyena_specs(row_count, tiles, most=STEP_TILES):
    group = math.gcd(tiles, most)
    return (
        (tiles // group,),
        pl.BlockSpec((row_count, group * LANES), lambda i: (0, i)),
        pl.BlockSpec((group, 1, LANES), lambda i: (i, 0, 0)),
        pl.BlockSpec((group, GROUP, LANES), lambda i: (i, 0, 0)),
    )


def local_part(gate_inner, gate_outer, hyena_value, rate, residue, skip_gain):
    row_count, chan_count = gate_inner.shape
    tiles = chan_count // LANES
    grid, wide, row, small = hyena_specs(row_count, tiles)
    return pl.pallas_call(
        local_kernel,
        grid=grid,
        in_specs=[wide, wide, wide, row, row, row],
        out_specs=[wide, small],
        out_shape=[
            jax.ShapeDtypeStruct((row_count, chan_count), F32),
            jax.ShapeDtypeStruct((tiles, GROUP, LANES), BF16),
        ],
        cost_estimate=pl.CostEstimate(
            flops=2 * row_count * chan_count * LANES * 16,
            bytes_accessed=10 * row_count * chan_count,
            transcendentals=row_count * chan_count,
        ),
        compiler_params=WHOLE_VMEM,
        name="local_part",
    )(gate_inner, gate_outer, hyena_value, rate, residue, skip_gain.reshape(tiles, 1, LANES))


def remote_part(where, part, gate_outer, rate, residue, before, other):
    row_count, chan_count = gate_outer.shape
    tiles = chan_count // LANES
    grid, wide, row, small = hyena_specs(row_count, tiles, 4)
    return pl.pallas_call(
        remote_kernel,
        grid=grid,
        in_specs=[pl.BlockSpec(memory_space=pltpu.SMEM), wide, wide, row, row, small, small],
        out_specs=wide,
        out_shape=jax.ShapeDtypeStruct((row_count, chan_count), BF16),
        cost_estimate=pl.CostEstimate(
            flops=2 * row_count * chan_count * LANES * 3,
            bytes_accessed=8 * row_count * chan_count,
            transcendentals=row_count * chan_count // 4,
        ),
        compiler_params=WHOLE_VMEM,
        name="remote_part",
    )(where, part, gate_outer, rate, residue, before, other)


def shifted(a, by, ctx_size):
    return lax.ppermute(a.astype(BF16), "ctx", [(i, i + by) for i in range(ctx_size - by)])


def scan_join(value, moved, base, rate, rows):
    for k, more in enumerate(moved, 1):
        value = value + more.astype(F32) * jnp.exp(-rate * float(rows * base * k))
    return value


def hyena_plain(gate_inner, gate_outer, hyena_value, modes, skip_gain, ctx_size):
    rate, residue = modes
    rows = gate_inner.shape[0]
    part, state = local_part(gate_inner, gate_outer, hyena_value, rate, residue, skip_gain)
    incoming = shifted(state, 1, ctx_size).astype(F32)
    base = 1
    while base < ctx_size - 1:
        incoming = scan_join(incoming, [shifted(incoming, base, ctx_size)], base, rate, rows)
        base *= 2
    where = jnp.zeros((1,), jnp.int32)
    return remote_part(
        where, part, gate_outer, rate, residue, incoming, jnp.zeros_like(state)
    )


def pack_kernel(place_ref, q_ref, k_ref, v_ref, *refs, spots, heads, head):
    outs, (buf, sems, out_sems) = refs[: len(spots)], refs[len(spots) :]
    place, rows = place_ref[0], q_ref.shape[0]
    reads = []
    for n, r in enumerate(spots):
        column = pl.multiple_of(((place ^ r) * heads + head) * HEAD_DIM, HEAD_DIM)
        for j, source in enumerate((q_ref, k_ref, v_ref)):
            reads.append(
                pltpu.make_async_copy(
                    source.at[:, pl.ds(column, HEAD_DIM)],
                    buf.at[n, pl.ds(j * rows, rows), :],
                    sems.at[n, j],
                )
            )
            reads[-1].start()
    writes = []
    for n in range(len(spots)):
        for j in range(3):
            reads[3 * n + j].wait()
        writes.append(pltpu.make_async_copy(buf.at[n], outs[n], out_sems.at[n]))
        writes[-1].start()
    for write in writes:
        write.wait()


def pack(place, arrays, spots, heads, head):
    rows = arrays[0].shape[0]
    shape = (3 * rows, HEAD_DIM)
    return pl.pallas_call(
        functools.partial(pack_kernel, spots=spots, heads=heads, head=head),
        in_specs=[pl.BlockSpec(memory_space=pltpu.SMEM)]
        + [pl.BlockSpec(memory_space=pl.ANY)] * 3,
        out_specs=[pl.BlockSpec(memory_space=pl.ANY)] * len(spots),
        out_shape=[jax.ShapeDtypeStruct(shape, BF16)] * len(spots),
        scratch_shapes=[
            pltpu.VMEM((len(spots),) + shape, BF16),
            pltpu.SemaphoreType.DMA((len(spots), 3)),
            pltpu.SemaphoreType.DMA((len(spots),)),
        ],
        cost_estimate=pl.CostEstimate(
            flops=0, bytes_accessed=4 * len(spots) * rows * 3 * HEAD_DIM, transcendentals=0
        ),
        compiler_params=WHOLE_VMEM,
        name="pack",
    )(place, *arrays)


def flash_kernel(place_ref, *refs, blocks):
    sources, outs = refs[:blocks], refs[blocks : 2 * blocks]
    q_buf, k_buf, v_buf, vt_buf, o_buf, l_buf, acc_buf, m_buf, sems = refs[2 * blocks :]
    rows = sources[0].shape[0] // 3
    place = place_ref[0]
    targets = (q_buf, k_buf, v_buf)

    def fetch(r, block, j):
        spot = pl.ds(pl.multiple_of(block * rows, rows), rows)
        return pltpu.make_async_copy(
            sources[r].at[pl.ds(j * rows, rows), :], targets[j].at[spot], sems.at[block, j]
        )

    for r in range(blocks):
        for j in range(3):
            fetch(r, place ^ r, j).start()

    def ready(block):
        for j in range(3):
            fetch(0, block, j).wait()
        spot = slice(block * rows, (block + 1) * rows)
        vt_buf[:, spot] = v_buf[spot, :].T

    scale = LOG2E / math.sqrt(HEAD_DIM)

    half, wide = rows // 2, 2 * rows
    ones = jnp.ones((8, HEAD_DIM), BF16)

    def squares(a):
        return mxu(ones, a * a, LAST)[:1]

    def lower(a):
        return jnp.where(iota(a.shape, 1) >= iota(a.shape, 0), a, floor_score)

    def jobs_of(i):
        jobs = [(j * rows, rows, 0, False) for j in range(2 * i)]
        for n in range(4):
            jobs.append((2 * i * rows + n * half, half, n * half, True))
        return jobs

    def score(i, job):
        start, count, first, masked = job
        scores = mxu(k_buf[start : start + count, :], q_buf[i * wide + first : (i + 1) * wide, :], LAST)
        if not masked:
            return scores
        head = lower(scores[:, :count])
        return head if first + count == wide else jnp.concatenate([head, scores[:, count:]], axis=1)

    key_square = jnp.zeros((1, rows), F32)
    smallest = jnp.full((1, wide), -floor_score, F32)
    for i in range(blocks // 2):
        for block in (2 * i, 2 * i + 1):
            ready(block)
            key_square = jnp.maximum(key_square, squares(k_buf[block * rows : (block + 1) * rows, :]))
        most = jnp.max(key_square, axis=1, keepdims=True)
        shift = jnp.sqrt(squares(q_buf[i * wide : (i + 1) * wide, :]) * most) * scale
        jobs = jobs_of(i)
        following = score(i, jobs[0])
        for n, (start, count, first, _) in enumerate(jobs):
            scores = following
            if n + 1 < len(jobs):
                following = score(i, jobs[n + 1])
            weights = jnp.exp2(scores * scale - shift[:, first:])
            total = jnp.sum(weights.reshape(count // 8, 8, wide - first), axis=0)
            update = mxu(vt_buf[:, start : start + count], weights.astype(BF16), PLAIN)
            if n == 0:
                acc_buf[i % 2] = update
                l_buf[i % 2] = total
            else:
                acc_buf[i % 2, :, first:] += update
                l_buf[i % 2, :, first:] += total
        total = jnp.sum(l_buf[i % 2], axis=0, keepdims=True)
        smallest = jnp.minimum(smallest, total)
        o_buf[i * wide : (i + 1) * wide, :] = (acc_buf[i % 2] / total).T.astype(BF16)

    @pl.when(jnp.min(smallest) < TOO_SMALL)
    def _():
        def one_query(i, carry):
            q_rows = pl.ds(pl.multiple_of(i * rows, rows), rows)
            m_buf[...] = jnp.full(m_buf.shape, floor_score, F32)
            l_buf[0, :, :rows] = jnp.zeros((8, rows), F32)
            acc_buf[0, :, :rows] = jnp.zeros((HEAD_DIM, rows), F32)

            def visit(j, masked):
                k_rows = pl.ds(pl.multiple_of(j * rows, rows), rows)
                scores = mxu(k_buf[k_rows, :], q_buf[q_rows, :], LAST)
                if masked:
                    scores = lower(scores)
                old = m_buf[:1, :]
                newest = jnp.maximum(old, jnp.max(scores, axis=0, keepdims=True) * scale)
                weights = jnp.exp2(scores * scale - newest)
                factor = jnp.exp2(old - newest)
                m_buf[:1, :] = newest
                l_buf[0, :, :rows] = l_buf[0, :, :rows] * factor + jnp.sum(
                    weights.reshape(rows // 8, 8, rows), axis=0
                )
                acc_buf[0, :, :rows] = acc_buf[0, :, :rows] * factor + mxu(
                    vt_buf[:, k_rows], weights.astype(BF16), PLAIN
                )

            def plain(j, inner):
                visit(j, False)
                return inner

            lax.fori_loop(0, i, plain, 0)
            visit(i, True)
            total = jnp.sum(l_buf[0, :, :rows], axis=0, keepdims=True)
            o_buf[q_rows, :] = (acc_buf[0, :, :rows] / total).T.astype(BF16)
            return carry

        lax.fori_loop(0, blocks, one_query, 0)

    writes = []
    for r in range(blocks):
        spot = pl.ds(pl.multiple_of((place ^ r) * rows, rows), rows)
        writes.append(pltpu.make_async_copy(o_buf.at[spot], outs[r], sems.at[r, 0]))
        writes[-1].start()
    for write in writes:
        write.wait()


def flash(place, sources):
    blocks, rows = len(sources), sources[0].shape[0] // 3
    total = blocks * rows
    pairs = total * (total + rows) // 2
    return pl.pallas_call(
        functools.partial(flash_kernel, blocks=blocks),
        in_specs=[pl.BlockSpec(memory_space=pltpu.SMEM)]
        + [pl.BlockSpec(memory_space=pl.ANY)] * blocks,
        out_specs=[pl.BlockSpec(memory_space=pl.ANY)] * blocks,
        out_shape=[jax.ShapeDtypeStruct((rows, HEAD_DIM), BF16)] * blocks,
        scratch_shapes=[
            pltpu.VMEM((total, HEAD_DIM), BF16),
            pltpu.VMEM((total, HEAD_DIM), BF16),
            pltpu.VMEM((total, HEAD_DIM), BF16),
            pltpu.VMEM((HEAD_DIM, total), BF16),
            pltpu.VMEM((total, HEAD_DIM), BF16),
            pltpu.VMEM((2, 8, 2 * rows), F32),
            pltpu.VMEM((2, HEAD_DIM, 2 * rows), F32),
            pltpu.VMEM((8, rows), F32),
            pltpu.SemaphoreType.DMA((blocks, 3)),
        ],
        compiler_params=WHOLE_VMEM,
        cost_estimate=pl.CostEstimate(
            flops=8 * pairs * HEAD_DIM, bytes_accessed=8 * total * HEAD_DIM, transcendentals=pairs
        ),
        name="flash",
    )(place, *sources)


def join_kernel(place_ref, *refs, blocks, heads):
    count = blocks * heads
    parts, out_ref, buf, sems = refs[:count], refs[-3], refs[-2], refs[-1]
    place = place_ref[0]
    reads, writes = [], []
    for n in range(count):
        reads.append(pltpu.make_async_copy(parts[n], buf.at[n], sems.at[0, n]))
        reads[-1].start()
    for n in range(count):
        column = pl.multiple_of(((place ^ (n % blocks)) * heads + n // blocks) * HEAD_DIM, HEAD_DIM)
        reads[n].wait()
        writes.append(
            pltpu.make_async_copy(buf.at[n], out_ref.at[:, pl.ds(column, HEAD_DIM)], sems.at[1, n])
        )
        writes[-1].start()
    for write in writes:
        write.wait()


def join(place, backs):
    heads, blocks = len(backs), len(backs[0])
    parts = [a for back in backs for a in back]
    rows = parts[0].shape[0]
    return pl.pallas_call(
        functools.partial(join_kernel, blocks=blocks, heads=heads),
        in_specs=[pl.BlockSpec(memory_space=pltpu.SMEM)]
        + [pl.BlockSpec(memory_space=pl.ANY)] * len(parts),
        out_specs=pl.BlockSpec(memory_space=pl.ANY),
        out_shape=jax.ShapeDtypeStruct((rows, blocks * heads * HEAD_DIM), BF16),
        scratch_shapes=[
            pltpu.VMEM((len(parts), rows, HEAD_DIM), BF16),
            pltpu.SemaphoreType.DMA((2, len(parts))),
        ],
        compiler_params=WHOLE_VMEM,
        cost_estimate=pl.CostEstimate(
            flops=0, bytes_accessed=4 * len(parts) * rows * HEAD_DIM, transcendentals=0
        ),
        name="join",
    )(place, *parts)


def exchange_body(
    gate_inner,
    gate_outer,
    hyena_value,
    decay_rate,
    residue,
    skip_gain,
    filter_index,
    query_rows,
    key_rows,
    value_rows,
    mesh,
):
    ctx_size, tp_size = mesh.shape["ctx"], mesh.shape["tp"]
    row_count, width_cols = query_rows.shape
    heads = width_cols // HEAD_DIM // ctx_size
    place = lax.axis_index("ctx")
    where = place.astype(jnp.int32).reshape(1)
    tiles = gate_inner.shape[1] // LANES

    def swap(a, r):
        return lax.ppermute(a, "ctx", [(i, i ^ r) for i in range(ctx_size)])

    order = list(SENDS) + [0]
    got, backs = [], []
    sent = query_rows
    lead = 2
    for h in range(heads):
        mine = [None] * ctx_size
        pieces = [order[:lead], order[lead:]] if h == 0 else [order]
        for some in pieces:
            packed = pack(where, (after(query_rows, sent), key_rows, value_rows), some, heads, h)
            sent = packed[0]
            for piece, r in zip(packed, some):
                mine[r] = swap(piece, r) if r else piece
        if h == 0:
            rate, local_residue = gathered_modes(
                decay_rate, residue, filter_index, tiles, tp_size, sent
            )
        got.append(mine)
    part, state = local_part(gate_inner, gate_outer, hyena_value, rate, local_residue, skip_gain)
    spot = jnp.stack([place.astype(jnp.int32), jnp.int32(row_count)])
    partner = swap(state, 1)
    (pair,) = state_call(pair_kernel, spot, rate, (state, partner), (BF16,))
    far = swap(pair, 2)
    for h in range(heads):
        results = flash(where, got[h])
        if h == heads - 2:
            far = after(far, results[0])
            before, total = state_call(gather_kernel, spot, rate, (partner, pair, far), (F32, BF16))
            other = swap(total, SPAN)
        back = list(results)
        for r in SENDS:
            back[r] = swap(results[r], r)
        backs.append(back)
    before = after(before, backs[-1][0])
    hyena_output = remote_part(where, part, gate_outer, rate, local_residue, before, other)
    backs[-1][0] = after(backs[-1][0], hyena_output)
    return (hyena_output, join(where, backs))


def row_steps(folded, members, handler, span_rows):
    total_rows = members[0].shape[0]
    block_count = total_rows // span_rows
    stacked = tuple(
        (member.reshape((block_count, span_rows) + member.shape[1:]) for member in members)
    )

    def advance(running, element):
        position, pieces = element
        return (handler(running, pieces, position * span_rows), None)

    folded, _ = lax.scan(advance, folded, (jnp.arange(block_count, dtype=jnp.int32), stacked))
    return folded


def gather_attention(query_rows, key_rows, value_rows):
    row_count, width_cols = query_rows.shape
    head_count = width_cols // HEAD_DIM
    queries = query_rows.reshape(row_count, head_count, HEAD_DIM)
    score_scale = 1.0 / math.sqrt(HEAD_DIM)
    own_rows = lax.axis_index("ctx") * row_count + jnp.arange(row_count, dtype=jnp.int32)

    def attend(folded, pieces, first_row):
        running_max, running_total, summed = folded
        block_rows = pieces[0].shape[0]
        keys_now = pieces[0].reshape(block_rows, head_count, HEAD_DIM)
        values_now = pieces[1].reshape(block_rows, head_count, HEAD_DIM)
        scores = (
            jnp.einsum("thd,shd->hts", queries, keys_now, preferred_element_type=jnp.float32)
            * score_scale
        )
        key_positions = first_row + jnp.arange(block_rows, dtype=jnp.int32)
        visible = own_rows[:, None] >= key_positions[None, :]
        masked = jnp.where(visible[None], scores, floor_score)
        newest = jnp.maximum(running_max, jnp.max(masked, axis=2))
        weights = jnp.where(visible[None], jnp.exp(scores - newest[:, :, None]), 0.0)
        factor = jnp.exp(running_max - newest)
        running_total = running_total * factor + jnp.sum(weights, axis=2)
        update = jnp.einsum(
            "hts,shd->thd",
            weights.astype(jnp.bfloat16),
            values_now,
            preferred_element_type=jnp.float32,
        )
        summed = summed * factor.T[:, :, None] + update
        return (newest, running_total, summed)

    initial = (
        jnp.full((head_count, row_count), floor_score, jnp.float32),
        jnp.zeros((head_count, row_count), jnp.float32),
        jnp.zeros((row_count, head_count, HEAD_DIM), jnp.float32),
    )
    _, running_total, summed = row_steps(
        initial,
        (
            lax.all_gather(key_rows, "ctx", axis=0, tiled=True),
            lax.all_gather(value_rows, "ctx", axis=0, tiled=True),
        ),
        attend,
        512,
    )
    result = summed / running_total.T[:, :, None]
    return result.reshape(row_count, width_cols).astype(jnp.bfloat16)


def solution(mesh):
    ctx_size, tp_size = mesh.shape["ctx"], mesh.shape["tp"]

    def body(
        gate_inner,
        gate_outer,
        hyena_value,
        decay_rate,
        residue,
        skip_gain,
        filter_index,
        query_rows,
        key_rows,
        value_rows,
    ):
        head_count = query_rows.shape[1] // HEAD_DIM
        if head_count % (2 * ctx_size) == 0 and ctx_size == 2 * SPAN:
            return exchange_body(
                gate_inner,
                gate_outer,
                hyena_value,
                decay_rate,
                residue,
                skip_gain,
                filter_index,
                query_rows,
                key_rows,
                value_rows,
                mesh,
            )
        attention_output = gather_attention(query_rows, key_rows, value_rows)
        tiles = gate_inner.shape[1] // LANES
        modes = gathered_modes(decay_rate, residue, filter_index, tiles, tp_size, None)
        hyena_output = hyena_plain(gate_inner, gate_outer, hyena_value, modes, skip_gain, ctx_size)
        return (hyena_output, attention_output)

    in_specs = (
        P("ctx", "tp"),
        P("ctx", "tp"),
        P("ctx", "tp"),
        P("tp", None),
        P("tp", None),
        P("tp"),
        P("tp"),
        P("ctx", "tp"),
        P("ctx", "tp"),
        P("ctx", "tp"),
    )
    out_specs = (P("ctx", "tp"), P("ctx", "tp"))
    return jax.shard_map(body, mesh=mesh, in_specs=in_specs, out_specs=out_specs, check_vma=False)
```

```python
import functools
import math

import jax
import jax.numpy as jnp
from jax import lax
from jax.experimental import pallas as pl
from jax.experimental.pallas import tpu as pltpu
from jax.sharding import PartitionSpec as P

HEAD_DIM = 128
GROUP = 16
LANES = 128
CHUNK = 128
TILE_GROUPS = LANES // GROUP
STEP_TILES = 4
SPAN = 4
SENDS = (6, 7, 4, 2, 5, 3, 1)
BACKS = (2, 4, 6, 7, 3, 5, 1)
WHOLE_VMEM = pltpu.CompilerParams(vmem_limit_bytes=63 << 20)

floor_score = -1e30
LOG2E = 1.4426950408889634
TOO_SMALL = 2.0**-80


F32 = jnp.float32
BF16 = jnp.bfloat16
LAST = (((1,), (1,)), ((), ()))
FIRST = (((0,), (0,)), ((), ()))
PLAIN = (((1,), (0,)), ((), ()))


def mxu(a, b, dims):
    return lax.dot_general(a, b, dims, preferred_element_type=F32)


def halves(a):
    high = a.astype(BF16)
    return high, (a - high.astype(F32)).astype(BF16)


def iota(shape, axis):
    return lax.broadcasted_iota(jnp.int32, shape, axis)


def same_group():
    rows, cols = iota((LANES, LANES), 0), iota((LANES, LANES), 1)
    return (rows // GROUP) == (cols // GROUP)


def carried_pieces(gate_ref, value_ref, lanes):
    rows = gate_ref.shape[0]
    carried = (gate_ref[:, lanes].astype(F32) * value_ref[:, lanes].astype(F32)).astype(BF16)
    return [carried[b * CHUNK : (b + 1) * CHUNK] for b in range(rows // CHUNK)]


def chunk_states(pieces, rate, step, mask):
    ends = jnp.concatenate(halves(jnp.exp((step - CHUNK) * rate)), axis=1)
    full = mxu(jnp.concatenate(pieces, axis=1), ends, FIRST)
    full = full[:, :LANES] + full[:, LANES:]
    return [
        jnp.where(mask, full[b * LANES : (b + 1) * LANES], 0.0) for b in range(len(pieces))
    ]


def spread_states(states, shrinking):
    state_high, state_low = halves(jnp.concatenate(states, axis=0))
    return mxu(
        jnp.concatenate(shrinking, axis=1),
        jnp.concatenate([state_high, state_high], axis=1),
        LAST,
    ) + mxu(shrinking[0], state_low, LAST)


def local_kernel(gate_ref, outer_ref, value_ref, rate_ref, residue_ref, skip_ref, out_ref, state_ref):
    cols = gate_ref.shape[1]
    step = iota((CHUNK, LANES), 0).astype(F32)
    lane_group = iota((CHUNK, LANES), 1) // GROUP
    zero = jnp.zeros((), BF16)
    shape = (CHUNK, TILE_GROUPS * CHUNK)
    causal = iota(shape, 0) >= iota(shape, 1) % CHUNK
    mask = same_group()
    pick = (iota((GROUP, LANES), 1) % GROUP == iota((GROUP, LANES), 0)).astype(BF16)

    def spread(a):
        return jnp.concatenate(
            [jnp.where(lane_group == g, a, zero) for g in range(TILE_GROUPS)], axis=0
        )

    for w in range(cols // LANES):
        lanes = slice(w * LANES, (w + 1) * LANES)
        rate, residue, skip = rate_ref[w], residue_ref[w], skip_ref[w]
        grown_high, grown_low = halves(jnp.exp((step - CHUNK // 2) * rate))
        shrunk = halves(residue * jnp.exp((CHUNK // 2 - step) * rate))
        from_start = halves(residue * jnp.exp(-step * rate))
        decay = jnp.exp(-CHUNK * rate)
        spread_high = spread(grown_high)
        taps = mxu(
            jnp.concatenate(shrunk, axis=1),
            jnp.concatenate([spread_high, spread_high], axis=1),
            LAST,
        ) + mxu(shrunk[0], spread(grown_low), LAST)
        toeplitz = jnp.where(causal, taps, 0.0).astype(BF16)
        pieces = carried_pieces(gate_ref, value_ref, lanes)
        blocks = jnp.concatenate(
            [
                jnp.concatenate(
                    [jnp.where(lane_group == g, piece, zero) for piece in pieces], axis=1
                )
                for g in range(TILE_GROUPS)
            ],
            axis=0,
        )
        inside = mxu(toeplitz, blocks, PLAIN)
        fresh = chunk_states(pieces, rate, step, mask)
        states = [fresh[0]]
        for more in fresh[1:]:
            states.append(states[-1] * decay + more)
        state_ref[w] = mxu(pick, states[-1].astype(BF16), PLAIN).astype(BF16)
        earlier = spread_states(states[:-1], from_start) if len(pieces) > 1 else None
        for b, piece in enumerate(pieces):
            convolved = inside[:, b * LANES : (b + 1) * LANES] + skip * piece.astype(F32)
            if b:
                convolved += earlier[:, (b - 1) * LANES : b * LANES]
            gate = outer_ref[b * CHUNK : (b + 1) * CHUNK, lanes].astype(F32)
            out_ref[b * CHUNK : (b + 1) * CHUNK, lanes] = gate * convolved


def pair_kernel(place_ref, rate_ref, mine_ref, other_ref, total_ref):
    mine, other = mine_ref[...].astype(F32), other_ref[...].astype(F32)
    second = place_ref[0] % 2 == 1
    lower, upper = jnp.where(second, other, mine), jnp.where(second, mine, other)
    rows = place_ref[1].astype(F32)
    total_ref[...] = (lower * jnp.exp(-rate_ref[...] * rows) + upper).astype(BF16)


def gather_kernel(place_ref, rate_ref, other_ref, pair_ref, far_ref, before_ref, total_ref):
    core, side = place_ref[0] % 2, (place_ref[0] // 2) % 2
    rows = place_ref[1].astype(F32)
    rate = rate_ref[...]
    pair, far = pair_ref[...].astype(F32), far_ref[...].astype(F32)
    faded = far * jnp.exp(-rate * (core.astype(F32) * rows))
    before_ref[...] = jnp.where(core == 1, other_ref[...].astype(F32), 0.0) + jnp.where(
        side == 1, faded, 0.0
    )
    lower, upper = jnp.where(side == 1, far, pair), jnp.where(side == 1, pair, far)
    total_ref[...] = (lower * jnp.exp(-rate * (2.0 * rows)) + upper).astype(BF16)


def state_call(kernel, where, rate, states, kinds):
    shape = states[0].shape
    return pl.pallas_call(
        kernel,
        in_specs=[pl.BlockSpec(memory_space=pltpu.SMEM)]
        + [pl.BlockSpec(memory_space=pltpu.VMEM)] * (1 + len(states)),
        out_specs=[pl.BlockSpec(memory_space=pltpu.VMEM)] * len(kinds),
        out_shape=[jax.ShapeDtypeStruct(shape, kind) for kind in kinds],
        compiler_params=WHOLE_VMEM,
    )(where, rate, *states)


def remote_kernel(
    place_ref, part_ref, outer_ref, rate_ref, residue_ref, before_ref, other_ref, out_ref
):
    rows, cols = outer_ref.shape
    step = iota((CHUNK, LANES), 0).astype(F32)
    mask = same_group()
    pick = (iota((LANES, GROUP), 0) % GROUP == iota((LANES, GROUP), 1)).astype(BF16)
    spot = (place_ref[0] % SPAN).astype(F32) * rows
    upper = place_ref[0] >= SPAN
    for w in range(cols // LANES):
        lanes = slice(w * LANES, (w + 1) * LANES)
        rate = rate_ref[w]
        faded = other_ref[w].astype(F32) * jnp.exp(-rate * spot)
        incoming = (before_ref[w] + jnp.where(upper, faded, 0.0)).astype(BF16)
        state = jnp.where(mask, mxu(pick, incoming, PLAIN), 0.0).astype(BF16)
        decay = jnp.exp(-CHUNK * rate)
        shrinking = [residue_ref[w] * jnp.exp(-step * rate)]
        while len(shrinking) < rows // CHUNK:
            shrinking.append(shrinking[-1] * decay)
        earlier = mxu(jnp.concatenate(shrinking, axis=0).astype(BF16), state, LAST)
        gate = outer_ref[:, lanes].astype(F32)
        out_ref[:, lanes] = (part_ref[:, lanes] + gate * earlier).astype(BF16)


def after(value, *earlier):
    return lax.optimization_barrier((value,) + earlier)[0]


def gathered_modes(decay_rate, residue, filter_index, tiles, tp_size, gate):
    modes = jnp.concatenate([decay_rate, residue], axis=1)
    if gate is not None:
        modes = after(modes, gate)
    filters, width = modes.shape
    if tp_size <= 4:
        place = lax.axis_index("tp")
        others = [modes] + [
            lax.ppermute(modes, "tp", [(i, (i + shift) % tp_size) for i in range(tp_size)])
            for shift in range(1, tp_size)
        ]
        bank = jnp.concatenate(others, axis=0)
        owner = filter_index // filters
        wanted = (place - owner) % tp_size * filters + filter_index % filters
    else:
        bank = lax.all_gather(modes, "tp", axis=0, tiled=True)
        wanted = filter_index
    chooser = (wanted[:, None] == jnp.arange(bank.shape[0], dtype=jnp.int32)[None, :]).astype(F32)
    local = jnp.dot(chooser, bank, precision=lax.Precision.HIGHEST)
    poles = width // 2
    return (
        local[:, :poles].reshape(tiles, 1, LANES),
        local[:, poles:].reshape(tiles, 1, LANES),
    )


def hyena_specs(row_count, tiles, most=STEP_TILES):
    group = math.gcd(tiles, most)
    return (
        (tiles // group,),
        pl.BlockSpec((row_count, group * LANES), lambda i: (0, i)),
        pl.BlockSpec((group, 1, LANES), lambda i: (i, 0, 0)),
        pl.BlockSpec((group, GROUP, LANES), lambda i: (i, 0, 0)),
    )


def local_part(gate_inner, gate_outer, hyena_value, rate, residue, skip_gain):
    row_count, chan_count = gate_inner.shape
    tiles = chan_count // LANES
    grid, wide, row, small = hyena_specs(row_count, tiles)
    return pl.pallas_call(
        local_kernel,
        grid=grid,
        in_specs=[wide, wide, wide, row, row, row],
        out_specs=[wide, small],
        out_shape=[
            jax.ShapeDtypeStruct((row_count, chan_count), F32),
            jax.ShapeDtypeStruct((tiles, GROUP, LANES), BF16),
        ],
        cost_estimate=pl.CostEstimate(
            flops=2 * row_count * chan_count * LANES * 16,
            bytes_accessed=10 * row_count * chan_count,
            transcendentals=row_count * chan_count,
        ),
        compiler_params=WHOLE_VMEM,
        name="local_part",
    )(gate_inner, gate_outer, hyena_value, rate, residue, skip_gain.reshape(tiles, 1, LANES))


def remote_part(where, part, gate_outer, rate, residue, before, other):
    row_count, chan_count = gate_outer.shape
    tiles = chan_count // LANES
    grid, wide, row, small = hyena_specs(row_count, tiles, 4)
    return pl.pallas_call(
        remote_kernel,
        grid=grid,
        in_specs=[pl.BlockSpec(memory_space=pltpu.SMEM), wide, wide, row, row, small, small],
        out_specs=wide,
        out_shape=jax.ShapeDtypeStruct((row_count, chan_count), BF16),
        cost_estimate=pl.CostEstimate(
            flops=2 * row_count * chan_count * LANES * 3,
            bytes_accessed=8 * row_count * chan_count,
            transcendentals=row_count * chan_count // 4,
        ),
        compiler_params=WHOLE_VMEM,
        name="remote_part",
    )(where, part, gate_outer, rate, residue, before, other)


def shifted(a, by, ctx_size):
    return lax.ppermute(a.astype(BF16), "ctx", [(i, i + by) for i in range(ctx_size - by)])


def scan_join(value, moved, base, rate, rows):
    for k, more in enumerate(moved, 1):
        value = value + more.astype(F32) * jnp.exp(-rate * float(rows * base * k))
    return value


def hyena_plain(gate_inner, gate_outer, hyena_value, modes, skip_gain, ctx_size):
    rate, residue = modes
    rows = gate_inner.shape[0]
    part, state = local_part(gate_inner, gate_outer, hyena_value, rate, residue, skip_gain)
    incoming = shifted(state, 1, ctx_size).astype(F32)
    base = 1
    while base < ctx_size - 1:
        incoming = scan_join(incoming, [shifted(incoming, base, ctx_size)], base, rate, rows)
        base *= 2
    where = jnp.zeros((1,), jnp.int32)
    return remote_part(
        where, part, gate_outer, rate, residue, incoming, jnp.zeros_like(state)
    )


def pack_kernel(place_ref, q_ref, k_ref, v_ref, *refs, spots, heads, head):
    outs, (buf, sems, out_sems) = refs[: len(spots)], refs[len(spots) :]
    place, rows = place_ref[0], q_ref.shape[0]
    reads = []
    for n, r in enumerate(spots):
        column = pl.multiple_of(((place ^ r) * heads + head) * HEAD_DIM, HEAD_DIM)
        for j, source in enumerate((q_ref, k_ref, v_ref)):
            reads.append(
                pltpu.make_async_copy(
                    source.at[:, pl.ds(column, HEAD_DIM)],
                    buf.at[n, pl.ds(j * rows, rows), :],
                    sems.at[n, j],
                )
            )
            reads[-1].start()
    writes = []
    for n in range(len(spots)):
        for j in range(3):
            reads[3 * n + j].wait()
        writes.append(pltpu.make_async_copy(buf.at[n], outs[n], out_sems.at[n]))
        writes[-1].start()
    for write in writes:
        write.wait()


def pack(place, arrays, spots, heads, head):
    rows = arrays[0].shape[0]
    shape = (3 * rows, HEAD_DIM)
    return pl.pallas_call(
        functools.partial(pack_kernel, spots=spots, heads=heads, head=head),
        in_specs=[pl.BlockSpec(memory_space=pltpu.SMEM)]
        + [pl.BlockSpec(memory_space=pl.ANY)] * 3,
        out_specs=[pl.BlockSpec(memory_space=pl.ANY)] * len(spots),
        out_shape=[jax.ShapeDtypeStruct(shape, BF16)] * len(spots),
        scratch_shapes=[
            pltpu.VMEM((len(spots),) + shape, BF16),
            pltpu.SemaphoreType.DMA((len(spots), 3)),
            pltpu.SemaphoreType.DMA((len(spots),)),
        ],
        cost_estimate=pl.CostEstimate(
            flops=0, bytes_accessed=4 * len(spots) * rows * 3 * HEAD_DIM, transcendentals=0
        ),
        compiler_params=WHOLE_VMEM,
        name="pack",
    )(place, *arrays)


def flash_kernel(place_ref, *refs, blocks):
    sources, outs = refs[:blocks], refs[blocks : 2 * blocks]
    q_buf, k_buf, v_buf, vt_buf, o_buf, l_buf, acc_buf, m_buf, sems = refs[2 * blocks :]
    rows = sources[0].shape[0] // 3
    place = place_ref[0]
    targets = (q_buf, k_buf, v_buf)

    def fetch(r, block, j):
        spot = pl.ds(pl.multiple_of(block * rows, rows), rows)
        return pltpu.make_async_copy(
            sources[r].at[pl.ds(j * rows, rows), :], targets[j].at[spot], sems.at[block, j]
        )

    for r in range(blocks):
        for j in range(3):
            fetch(r, place ^ r, j).start()

    def ready(block):
        for j in range(3):
            fetch(0, block, j).wait()
        spot = slice(block * rows, (block + 1) * rows)
        vt_buf[:, spot] = v_buf[spot, :].T

    scale = LOG2E / math.sqrt(HEAD_DIM)

    half, wide = rows // 2, 2 * rows
    ones = jnp.ones((8, HEAD_DIM), BF16)

    def squares(a):
        return mxu(ones, a * a, LAST)[:1]

    def lower(a):
        return jnp.where(iota(a.shape, 1) >= iota(a.shape, 0), a, floor_score)

    def jobs_of(i):
        jobs = [(j * rows, rows, 0, False) for j in range(2 * i)]
        for n in range(4):
            jobs.append((2 * i * rows + n * half, half, n * half, True))
        return jobs

    def score(i, job):
        start, count, first, masked = job
        scores = mxu(k_buf[start : start + count, :], q_buf[i * wide + first : (i + 1) * wide, :], LAST)
        if not masked:
            return scores
        head = lower(scores[:, :count])
        return head if first + count == wide else jnp.concatenate([head, scores[:, count:]], axis=1)

    key_square = jnp.zeros((1, rows), F32)
    smallest = jnp.full((1, wide), -floor_score, F32)
    for i in range(blocks // 2):
        for block in (2 * i, 2 * i + 1):
            ready(block)
            key_square = jnp.maximum(key_square, squares(k_buf[block * rows : (block + 1) * rows, :]))
        most = jnp.max(key_square, axis=1, keepdims=True)
        shift = jnp.sqrt(squares(q_buf[i * wide : (i + 1) * wide, :]) * most) * scale
        jobs = jobs_of(i)
        following = score(i, jobs[0])
        for n, (start, count, first, _) in enumerate(jobs):
            scores = following
            if n + 1 < len(jobs):
                following = score(i, jobs[n + 1])
            weights = jnp.exp2(scores * scale - shift[:, first:])
            total = jnp.sum(weights.reshape(count // 8, 8, wide - first), axis=0)
            update = mxu(vt_buf[:, start : start + count], weights.astype(BF16), PLAIN)
            if n == 0:
                acc_buf[i % 2] = update
                l_buf[i % 2] = total
            else:
                acc_buf[i % 2, :, first:] += update
                l_buf[i % 2, :, first:] += total
        total = jnp.sum(l_buf[i % 2], axis=0, keepdims=True)
        smallest = jnp.minimum(smallest, total)
        o_buf[i * wide : (i + 1) * wide, :] = (acc_buf[i % 2] / total).T.astype(BF16)

    @pl.when(jnp.min(smallest) < TOO_SMALL)
    def _():
        def one_query(i, carry):
            q_rows = pl.ds(pl.multiple_of(i * rows, rows), rows)
            m_buf[...] = jnp.full(m_buf.shape, floor_score, F32)
            l_buf[0, :, :rows] = jnp.zeros((8, rows), F32)
            acc_buf[0, :, :rows] = jnp.zeros((HEAD_DIM, rows), F32)

            def visit(j, masked):
                k_rows = pl.ds(pl.multiple_of(j * rows, rows), rows)
                scores = mxu(k_buf[k_rows, :], q_buf[q_rows, :], LAST)
                if masked:
                    scores = lower(scores)
                old = m_buf[:1, :]
                newest = jnp.maximum(old, jnp.max(scores, axis=0, keepdims=True) * scale)
                weights = jnp.exp2(scores * scale - newest)
                factor = jnp.exp2(old - newest)
                m_buf[:1, :] = newest
                l_buf[0, :, :rows] = l_buf[0, :, :rows] * factor + jnp.sum(
                    weights.reshape(rows // 8, 8, rows), axis=0
                )
                acc_buf[0, :, :rows] = acc_buf[0, :, :rows] * factor + mxu(
                    vt_buf[:, k_rows], weights.astype(BF16), PLAIN
                )

            def plain(j, inner):
                visit(j, False)
                return inner

            lax.fori_loop(0, i, plain, 0)
            visit(i, True)
            total = jnp.sum(l_buf[0, :, :rows], axis=0, keepdims=True)
            o_buf[q_rows, :] = (acc_buf[0, :, :rows] / total).T.astype(BF16)
            return carry

        lax.fori_loop(0, blocks, one_query, 0)

    writes = []
    for r in range(blocks):
        spot = pl.ds(pl.multiple_of((place ^ r) * rows, rows), rows)
        writes.append(pltpu.make_async_copy(o_buf.at[spot], outs[r], sems.at[r, 0]))
        writes[-1].start()
    for write in writes:
        write.wait()


def flash(place, sources):
    blocks, rows = len(sources), sources[0].shape[0] // 3
    total = blocks * rows
    pairs = total * (total + rows) // 2
    return pl.pallas_call(
        functools.partial(flash_kernel, blocks=blocks),
        in_specs=[pl.BlockSpec(memory_space=pltpu.SMEM)]
        + [pl.BlockSpec(memory_space=pl.ANY)] * blocks,
        out_specs=[pl.BlockSpec(memory_space=pl.ANY)] * blocks,
        out_shape=[jax.ShapeDtypeStruct((rows, HEAD_DIM), BF16)] * blocks,
        scratch_shapes=[
            pltpu.VMEM((total, HEAD_DIM), BF16),
            pltpu.VMEM((total, HEAD_DIM), BF16),
            pltpu.VMEM((total, HEAD_DIM), BF16),
            pltpu.VMEM((HEAD_DIM, total), BF16),
            pltpu.VMEM((total, HEAD_DIM), BF16),
            pltpu.VMEM((2, 8, 2 * rows), F32),
            pltpu.VMEM((2, HEAD_DIM, 2 * rows), F32),
            pltpu.VMEM((8, rows), F32),
            pltpu.SemaphoreType.DMA((blocks, 3)),
        ],
        compiler_params=WHOLE_VMEM,
        cost_estimate=pl.CostEstimate(
            flops=8 * pairs * HEAD_DIM, bytes_accessed=8 * total * HEAD_DIM, transcendentals=pairs
        ),
        name="flash",
    )(place, *sources)


def join_kernel(place_ref, *refs, blocks, heads):
    count = blocks * heads
    parts, out_ref, buf, sems = refs[:count], refs[-3], refs[-2], refs[-1]
    place = place_ref[0]
    reads, writes = [], []
    for n in range(count):
        reads.append(pltpu.make_async_copy(parts[n], buf.at[n], sems.at[0, n]))
        reads[-1].start()
    for n in range(count):
        column = pl.multiple_of(((place ^ (n % blocks)) * heads + n // blocks) * HEAD_DIM, HEAD_DIM)
        reads[n].wait()
        writes.append(
            pltpu.make_async_copy(buf.at[n], out_ref.at[:, pl.ds(column, HEAD_DIM)], sems.at[1, n])
        )
        writes[-1].start()
    for write in writes:
        write.wait()


def join(place, backs):
    heads, blocks = len(backs), len(backs[0])
    parts = [a for back in backs for a in back]
    rows = parts[0].shape[0]
    return pl.pallas_call(
        functools.partial(join_kernel, blocks=blocks, heads=heads),
        in_specs=[pl.BlockSpec(memory_space=pltpu.SMEM)]
        + [pl.BlockSpec(memory_space=pl.ANY)] * len(parts),
        out_specs=pl.BlockSpec(memory_space=pl.ANY),
        out_shape=jax.ShapeDtypeStruct((rows, blocks * heads * HEAD_DIM), BF16),
        scratch_shapes=[
            pltpu.VMEM((len(parts), rows, HEAD_DIM), BF16),
            pltpu.SemaphoreType.DMA((2, len(parts))),
        ],
        compiler_params=WHOLE_VMEM,
        cost_estimate=pl.CostEstimate(
            flops=0, bytes_accessed=4 * len(parts) * rows * HEAD_DIM, transcendentals=0
        ),
        name="join",
    )(place, *parts)


def exchange_body(
    gate_inner,
    gate_outer,
    hyena_value,
    decay_rate,
    residue,
    skip_gain,
    filter_index,
    query_rows,
    key_rows,
    value_rows,
    mesh,
):
    ctx_size, tp_size = mesh.shape["ctx"], mesh.shape["tp"]
    row_count, width_cols = query_rows.shape
    heads = width_cols // HEAD_DIM // ctx_size
    place = lax.axis_index("ctx")
    where = place.astype(jnp.int32).reshape(1)
    tiles = gate_inner.shape[1] // LANES

    def swap(a, r):
        return lax.ppermute(a, "ctx", [(i, i ^ r) for i in range(ctx_size)])

    order = list(SENDS) + [0]
    got, backs = [], []
    sent = query_rows
    lead = 1
    for h in range(heads):
        mine = [None] * ctx_size
        pieces = [order[:lead], order[lead:]] if h == 0 else [order]
        for some in pieces:
            packed = pack(where, (after(query_rows, sent), key_rows, value_rows), some, heads, h)
            sent = packed[0]
            for piece, r in zip(packed, some):
                mine[r] = swap(piece, r) if r else piece
        if h == 0:
            rate, local_residue = gathered_modes(
                decay_rate, residue, filter_index, tiles, tp_size, sent
            )
        got.append(mine)
    part, state = local_part(gate_inner, gate_outer, hyena_value, rate, local_residue, skip_gain)
    spot = jnp.stack([place.astype(jnp.int32), jnp.int32(row_count)])
    partner = swap(state, 1)
    (pair,) = state_call(pair_kernel, spot, rate, (state, partner), (BF16,))
    far = swap(pair, 2)
    for h in range(heads):
        results = flash(where, got[h])
        if h == heads - 2:
            far = after(far, results[0])
            before, total = state_call(gather_kernel, spot, rate, (partner, pair, far), (F32, BF16))
            other = swap(total, SPAN)
        back = list(results)
        for r in BACKS:
            back[r] = swap(results[r], r)
        backs.append(back)
    before = after(before, backs[-1][0])
    hyena_output = remote_part(where, part, gate_outer, rate, local_residue, before, other)
    backs[-1][0] = after(backs[-1][0], hyena_output)
    return (hyena_output, join(where, backs))


def row_steps(folded, members, handler, span_rows):
    total_rows = members[0].shape[0]
    block_count = total_rows // span_rows
    stacked = tuple(
        (member.reshape((block_count, span_rows) + member.shape[1:]) for member in members)
    )

    def advance(running, element):
        position, pieces = element
        return (handler(running, pieces, position * span_rows), None)

    folded, _ = lax.scan(advance, folded, (jnp.arange(block_count, dtype=jnp.int32), stacked))
    return folded


def gather_attention(query_rows, key_rows, value_rows):
    row_count, width_cols = query_rows.shape
    head_count = width_cols // HEAD_DIM
    queries = query_rows.reshape(row_count, head_count, HEAD_DIM)
    score_scale = 1.0 / math.sqrt(HEAD_DIM)
    own_rows = lax.axis_index("ctx") * row_count + jnp.arange(row_count, dtype=jnp.int32)

    def attend(folded, pieces, first_row):
        running_max, running_total, summed = folded
        block_rows = pieces[0].shape[0]
        keys_now = pieces[0].reshape(block_rows, head_count, HEAD_DIM)
        values_now = pieces[1].reshape(block_rows, head_count, HEAD_DIM)
        scores = (
            jnp.einsum("thd,shd->hts", queries, keys_now, preferred_element_type=jnp.float32)
            * score_scale
        )
        key_positions = first_row + jnp.arange(block_rows, dtype=jnp.int32)
        visible = own_rows[:, None] >= key_positions[None, :]
        masked = jnp.where(visible[None], scores, floor_score)
        newest = jnp.maximum(running_max, jnp.max(masked, axis=2))
        weights = jnp.where(visible[None], jnp.exp(scores - newest[:, :, None]), 0.0)
        factor = jnp.exp(running_max - newest)
        running_total = running_total * factor + jnp.sum(weights, axis=2)
        update = jnp.einsum(
            "hts,shd->thd",
            weights.astype(jnp.bfloat16),
            values_now,
            preferred_element_type=jnp.float32,
        )
        summed = summed * factor.T[:, :, None] + update
        return (newest, running_total, summed)

    initial = (
        jnp.full((head_count, row_count), floor_score, jnp.float32),
        jnp.zeros((head_count, row_count), jnp.float32),
        jnp.zeros((row_count, head_count, HEAD_DIM), jnp.float32),
    )
    _, running_total, summed = row_steps(
        initial,
        (
            lax.all_gather(key_rows, "ctx", axis=0, tiled=True),
            lax.all_gather(value_rows, "ctx", axis=0, tiled=True),
        ),
        attend,
        512,
    )
    result = summed / running_total.T[:, :, None]
    return result.reshape(row_count, width_cols).astype(jnp.bfloat16)


def solution(mesh):
    ctx_size, tp_size = mesh.shape["ctx"], mesh.shape["tp"]

    def body(
        gate_inner,
        gate_outer,
        hyena_value,
        decay_rate,
        residue,
        skip_gain,
        filter_index,
        query_rows,
        key_rows,
        value_rows,
    ):
        head_count = query_rows.shape[1] // HEAD_DIM
        if head_count % (2 * ctx_size) == 0 and ctx_size == 2 * SPAN:
            return exchange_body(
                gate_inner,
                gate_outer,
                hyena_value,
                decay_rate,
                residue,
                skip_gain,
                filter_index,
                query_rows,
                key_rows,
                value_rows,
                mesh,
            )
        attention_output = gather_attention(query_rows, key_rows, value_rows)
        tiles = gate_inner.shape[1] // LANES
        modes = gathered_modes(decay_rate, residue, filter_index, tiles, tp_size, None)
        hyena_output = hyena_plain(gate_inner, gate_outer, hyena_value, modes, skip_gain, ctx_size)
        return (hyena_output, attention_output)

    in_specs = (
        P("ctx", "tp"),
        P("ctx", "tp"),
        P("ctx", "tp"),
        P("tp", None),
        P("tp", None),
        P("tp"),
        P("tp"),
        P("ctx", "tp"),
        P("ctx", "tp"),
        P("ctx", "tp"),
    )
    out_specs = (P("ctx", "tp"), P("ctx", "tp"))
    return jax.shard_map(body, mesh=mesh, in_specs=in_specs, out_specs=out_specs, check_vma=False)
```

```python
import functools
import math

import jax
import jax.numpy as jnp
from jax import lax
from jax.experimental import pallas as pl
from jax.experimental.pallas import tpu as pltpu
from jax.sharding import PartitionSpec as P

HEAD_DIM = 128
GROUP = 16
LANES = 128
CHUNK = 128
TILE_GROUPS = LANES // GROUP
STEP_TILES = 4
SPAN = 4
SENDS = (6, 7, 4, 2, 5, 3, 1)
BACKS = (2, 4, 6, 7, 3, 5, 1)
WHOLE_VMEM = pltpu.CompilerParams(vmem_limit_bytes=63 << 20)

floor_score = -1e30
LOG2E = 1.4426950408889634
TOO_SMALL = 2.0**-80
AHEAD = 2


F32 = jnp.float32
BF16 = jnp.bfloat16
LAST = (((1,), (1,)), ((), ()))
FIRST = (((0,), (0,)), ((), ()))
PLAIN = (((1,), (0,)), ((), ()))


def mxu(a, b, dims):
    return lax.dot_general(a, b, dims, preferred_element_type=F32)


def halves(a):
    high = a.astype(BF16)
    return high, (a - high.astype(F32)).astype(BF16)


def iota(shape, axis):
    return lax.broadcasted_iota(jnp.int32, shape, axis)


def same_group():
    rows, cols = iota((LANES, LANES), 0), iota((LANES, LANES), 1)
    return (rows // GROUP) == (cols // GROUP)


def carried_pieces(gate_ref, value_ref, lanes):
    rows = gate_ref.shape[0]
    carried = (gate_ref[:, lanes].astype(F32) * value_ref[:, lanes].astype(F32)).astype(BF16)
    return [carried[b * CHUNK : (b + 1) * CHUNK] for b in range(rows // CHUNK)]


def chunk_states(pieces, rate, step, mask):
    ends = jnp.concatenate(halves(jnp.exp((step - CHUNK) * rate)), axis=1)
    full = mxu(jnp.concatenate(pieces, axis=1), ends, FIRST)
    full = full[:, :LANES] + full[:, LANES:]
    return [
        jnp.where(mask, full[b * LANES : (b + 1) * LANES], 0.0) for b in range(len(pieces))
    ]


def spread_states(states, shrinking):
    state_high, state_low = halves(jnp.concatenate(states, axis=0))
    return mxu(
        jnp.concatenate(shrinking, axis=1),
        jnp.concatenate([state_high, state_high], axis=1),
        LAST,
    ) + mxu(shrinking[0], state_low, LAST)


def local_kernel(gate_ref, outer_ref, value_ref, rate_ref, residue_ref, skip_ref, out_ref, state_ref):
    cols = gate_ref.shape[1]
    step = iota((CHUNK, LANES), 0).astype(F32)
    lane_group = iota((CHUNK, LANES), 1) // GROUP
    zero = jnp.zeros((), BF16)
    shape = (CHUNK, TILE_GROUPS * CHUNK)
    causal = iota(shape, 0) >= iota(shape, 1) % CHUNK
    mask = same_group()
    pick = (iota((GROUP, LANES), 1) % GROUP == iota((GROUP, LANES), 0)).astype(BF16)

    def spread(a):
        return jnp.concatenate(
            [jnp.where(lane_group == g, a, zero) for g in range(TILE_GROUPS)], axis=0
        )

    for w in range(cols // LANES):
        lanes = slice(w * LANES, (w + 1) * LANES)
        rate, residue, skip = rate_ref[w], residue_ref[w], skip_ref[w]
        grown_high, grown_low = halves(jnp.exp((step - CHUNK // 2) * rate))
        shrunk = halves(residue * jnp.exp((CHUNK // 2 - step) * rate))
        from_start = halves(residue * jnp.exp(-step * rate))
        decay = jnp.exp(-CHUNK * rate)
        spread_high = spread(grown_high)
        taps = mxu(
            jnp.concatenate(shrunk, axis=1),
            jnp.concatenate([spread_high, spread_high], axis=1),
            LAST,
        ) + mxu(shrunk[0], spread(grown_low), LAST)
        toeplitz = jnp.where(causal, taps, 0.0).astype(BF16)
        pieces = carried_pieces(gate_ref, value_ref, lanes)
        blocks = jnp.concatenate(
            [
                jnp.concatenate(
                    [jnp.where(lane_group == g, piece, zero) for piece in pieces], axis=1
                )
                for g in range(TILE_GROUPS)
            ],
            axis=0,
        )
        inside = mxu(toeplitz, blocks, PLAIN)
        fresh = chunk_states(pieces, rate, step, mask)
        states = [fresh[0]]
        for more in fresh[1:]:
            states.append(states[-1] * decay + more)
        state_ref[w] = mxu(pick, states[-1].astype(BF16), PLAIN).astype(BF16)
        earlier = spread_states(states[:-1], from_start) if len(pieces) > 1 else None
        for b, piece in enumerate(pieces):
            convolved = inside[:, b * LANES : (b + 1) * LANES] + skip * piece.astype(F32)
            if b:
                convolved += earlier[:, (b - 1) * LANES : b * LANES]
            gate = outer_ref[b * CHUNK : (b + 1) * CHUNK, lanes].astype(F32)
            out_ref[b * CHUNK : (b + 1) * CHUNK, lanes] = gate * convolved


def pair_kernel(place_ref, rate_ref, mine_ref, other_ref, total_ref):
    mine, other = mine_ref[...].astype(F32), other_ref[...].astype(F32)
    second = place_ref[0] % 2 == 1
    lower, upper = jnp.where(second, other, mine), jnp.where(second, mine, other)
    rows = place_ref[1].astype(F32)
    total_ref[...] = (lower * jnp.exp(-rate_ref[...] * rows) + upper).astype(BF16)


def gather_kernel(place_ref, rate_ref, other_ref, pair_ref, far_ref, before_ref, total_ref):
    core, side = place_ref[0] % 2, (place_ref[0] // 2) % 2
    rows = place_ref[1].astype(F32)
    rate = rate_ref[...]
    pair, far = pair_ref[...].astype(F32), far_ref[...].astype(F32)
    faded = far * jnp.exp(-rate * (core.astype(F32) * rows))
    before_ref[...] = jnp.where(core == 1, other_ref[...].astype(F32), 0.0) + jnp.where(
        side == 1, faded, 0.0
    )
    lower, upper = jnp.where(side == 1, far, pair), jnp.where(side == 1, pair, far)
    total_ref[...] = (lower * jnp.exp(-rate * (2.0 * rows)) + upper).astype(BF16)


def state_call(kernel, where, rate, states, kinds):
    shape = states[0].shape
    return pl.pallas_call(
        kernel,
        in_specs=[pl.BlockSpec(memory_space=pltpu.SMEM)]
        + [pl.BlockSpec(memory_space=pltpu.VMEM)] * (1 + len(states)),
        out_specs=[pl.BlockSpec(memory_space=pltpu.VMEM)] * len(kinds),
        out_shape=[jax.ShapeDtypeStruct(shape, kind) for kind in kinds],
        compiler_params=WHOLE_VMEM,
    )(where, rate, *states)


def remote_kernel(
    place_ref, part_ref, outer_ref, rate_ref, residue_ref, before_ref, other_ref, out_ref
):
    rows, cols = outer_ref.shape
    step = iota((CHUNK, LANES), 0).astype(F32)
    mask = same_group()
    pick = (iota((LANES, GROUP), 0) % GROUP == iota((LANES, GROUP), 1)).astype(BF16)
    spot = (place_ref[0] % SPAN).astype(F32) * rows
    upper = place_ref[0] >= SPAN
    for w in range(cols // LANES):
        lanes = slice(w * LANES, (w + 1) * LANES)
        rate = rate_ref[w]
        faded = other_ref[w].astype(F32) * jnp.exp(-rate * spot)
        incoming = (before_ref[w] + jnp.where(upper, faded, 0.0)).astype(BF16)
        state = jnp.where(mask, mxu(pick, incoming, PLAIN), 0.0).astype(BF16)
        decay = jnp.exp(-CHUNK * rate)
        shrinking = [residue_ref[w] * jnp.exp(-step * rate)]
        while len(shrinking) < rows // CHUNK:
            shrinking.append(shrinking[-1] * decay)
        earlier = mxu(jnp.concatenate(shrinking, axis=0).astype(BF16), state, LAST)
        gate = outer_ref[:, lanes].astype(F32)
        out_ref[:, lanes] = (part_ref[:, lanes] + gate * earlier).astype(BF16)


def after(value, *earlier):
    return lax.optimization_barrier((value,) + earlier)[0]


def gathered_modes(decay_rate, residue, filter_index, tiles, tp_size, gate):
    modes = jnp.concatenate([decay_rate, residue], axis=1)
    if gate is not None:
        modes = after(modes, gate)
    filters, width = modes.shape
    if tp_size <= 4:
        place = lax.axis_index("tp")
        others = [modes] + [
            lax.ppermute(modes, "tp", [(i, (i + shift) % tp_size) for i in range(tp_size)])
            for shift in range(1, tp_size)
        ]
        bank = jnp.concatenate(others, axis=0)
        owner = filter_index // filters
        wanted = (place - owner) % tp_size * filters + filter_index % filters
    else:
        bank = lax.all_gather(modes, "tp", axis=0, tiled=True)
        wanted = filter_index
    chooser = (wanted[:, None] == jnp.arange(bank.shape[0], dtype=jnp.int32)[None, :]).astype(F32)
    local = jnp.dot(chooser, bank, precision=lax.Precision.HIGHEST)
    poles = width // 2
    return (
        local[:, :poles].reshape(tiles, 1, LANES),
        local[:, poles:].reshape(tiles, 1, LANES),
    )


def hyena_specs(row_count, tiles, most=STEP_TILES):
    group = math.gcd(tiles, most)
    return (
        (tiles // group,),
        pl.BlockSpec((row_count, group * LANES), lambda i: (0, i)),
        pl.BlockSpec((group, 1, LANES), lambda i: (i, 0, 0)),
        pl.BlockSpec((group, GROUP, LANES), lambda i: (i, 0, 0)),
    )


def local_part(gate_inner, gate_outer, hyena_value, rate, residue, skip_gain):
    row_count, chan_count = gate_inner.shape
    tiles = chan_count // LANES
    grid, wide, row, small = hyena_specs(row_count, tiles)
    return pl.pallas_call(
        local_kernel,
        grid=grid,
        in_specs=[wide, wide, wide, row, row, row],
        out_specs=[wide, small],
        out_shape=[
            jax.ShapeDtypeStruct((row_count, chan_count), F32),
            jax.ShapeDtypeStruct((tiles, GROUP, LANES), BF16),
        ],
        cost_estimate=pl.CostEstimate(
            flops=2 * row_count * chan_count * LANES * 16,
            bytes_accessed=10 * row_count * chan_count,
            transcendentals=row_count * chan_count,
        ),
        compiler_params=WHOLE_VMEM,
        name="local_part",
    )(gate_inner, gate_outer, hyena_value, rate, residue, skip_gain.reshape(tiles, 1, LANES))


def remote_part(where, part, gate_outer, rate, residue, before, other):
    row_count, chan_count = gate_outer.shape
    tiles = chan_count // LANES
    grid, wide, row, small = hyena_specs(row_count, tiles, 4)
    return pl.pallas_call(
        remote_kernel,
        grid=grid,
        in_specs=[pl.BlockSpec(memory_space=pltpu.SMEM), wide, wide, row, row, small, small],
        out_specs=wide,
        out_shape=jax.ShapeDtypeStruct((row_count, chan_count), BF16),
        cost_estimate=pl.CostEstimate(
            flops=2 * row_count * chan_count * LANES * 3,
            bytes_accessed=8 * row_count * chan_count,
            transcendentals=row_count * chan_count // 4,
        ),
        compiler_params=WHOLE_VMEM,
        name="remote_part",
    )(where, part, gate_outer, rate, residue, before, other)


def shifted(a, by, ctx_size):
    return lax.ppermute(a.astype(BF16), "ctx", [(i, i + by) for i in range(ctx_size - by)])


def scan_join(value, moved, base, rate, rows):
    for k, more in enumerate(moved, 1):
        value = value + more.astype(F32) * jnp.exp(-rate * float(rows * base * k))
    return value


def hyena_plain(gate_inner, gate_outer, hyena_value, modes, skip_gain, ctx_size):
    rate, residue = modes
    rows = gate_inner.shape[0]
    part, state = local_part(gate_inner, gate_outer, hyena_value, rate, residue, skip_gain)
    incoming = shifted(state, 1, ctx_size).astype(F32)
    base = 1
    while base < ctx_size - 1:
        incoming = scan_join(incoming, [shifted(incoming, base, ctx_size)], base, rate, rows)
        base *= 2
    where = jnp.zeros((1,), jnp.int32)
    return remote_part(
        where, part, gate_outer, rate, residue, incoming, jnp.zeros_like(state)
    )


def pack_kernel(place_ref, q_ref, k_ref, v_ref, *refs, spots, heads, head):
    outs, (buf, sems, out_sems) = refs[: len(spots)], refs[len(spots) :]
    place, rows = place_ref[0], q_ref.shape[0]
    reads = []
    for n, r in enumerate(spots):
        column = pl.multiple_of(((place ^ r) * heads + head) * HEAD_DIM, HEAD_DIM)
        for j, source in enumerate((q_ref, k_ref, v_ref)):
            reads.append(
                pltpu.make_async_copy(
                    source.at[:, pl.ds(column, HEAD_DIM)],
                    buf.at[n, pl.ds(j * rows, rows), :],
                    sems.at[n, j],
                )
            )
            reads[-1].start()
    writes = []
    for n in range(len(spots)):
        for j in range(3):
            reads[3 * n + j].wait()
        writes.append(pltpu.make_async_copy(buf.at[n], outs[n], out_sems.at[n]))
        writes[-1].start()
    for write in writes:
        write.wait()


def pack(place, arrays, spots, heads, head):
    rows = arrays[0].shape[0]
    shape = (3 * rows, HEAD_DIM)
    return pl.pallas_call(
        functools.partial(pack_kernel, spots=spots, heads=heads, head=head),
        in_specs=[pl.BlockSpec(memory_space=pltpu.SMEM)]
        + [pl.BlockSpec(memory_space=pl.ANY)] * 3,
        out_specs=[pl.BlockSpec(memory_space=pl.ANY)] * len(spots),
        out_shape=[jax.ShapeDtypeStruct(shape, BF16)] * len(spots),
        scratch_shapes=[
            pltpu.VMEM((len(spots),) + shape, BF16),
            pltpu.SemaphoreType.DMA((len(spots), 3)),
            pltpu.SemaphoreType.DMA((len(spots),)),
        ],
        cost_estimate=pl.CostEstimate(
            flops=0, bytes_accessed=4 * len(spots) * rows * 3 * HEAD_DIM, transcendentals=0
        ),
        compiler_params=WHOLE_VMEM,
        name="pack",
    )(place, *arrays)


def flash_kernel(place_ref, *refs, blocks):
    sources, outs = refs[:blocks], refs[blocks : 2 * blocks]
    q_buf, k_buf, v_buf, vt_buf, o_buf, l_buf, acc_buf, m_buf, sems = refs[2 * blocks :]
    rows = sources[0].shape[0] // 3
    place = place_ref[0]
    targets = (q_buf, k_buf, v_buf)

    def fetch(r, block, j):
        spot = pl.ds(pl.multiple_of(block * rows, rows), rows)
        return pltpu.make_async_copy(
            sources[r].at[pl.ds(j * rows, rows), :], targets[j].at[spot], sems.at[block, j]
        )

    for r in range(blocks):
        for j in range(3):
            fetch(r, place ^ r, j).start()

    def ready(block):
        for j in range(3):
            fetch(0, block, j).wait()
        spot = slice(block * rows, (block + 1) * rows)
        vt_buf[:, spot] = v_buf[spot, :].T

    scale = LOG2E / math.sqrt(HEAD_DIM)

    half, wide = rows // 2, 2 * rows
    ones = jnp.ones((8, HEAD_DIM), BF16)

    def squares(a):
        return mxu(ones, a * a, LAST)[:1]

    def lower(a):
        return jnp.where(iota(a.shape, 1) >= iota(a.shape, 0), a, floor_score)

    def jobs_of(i):
        jobs = [(j * rows, rows, 0, False) for j in range(2 * i)]
        for n in range(4):
            jobs.append((2 * i * rows + n * half, half, n * half, True))
        return jobs

    def score(i, job):
        start, count, first, masked = job
        scores = mxu(k_buf[start : start + count, :], q_buf[i * wide + first : (i + 1) * wide, :], LAST)
        if not masked:
            return scores
        head = lower(scores[:, :count])
        return head if first + count == wide else jnp.concatenate([head, scores[:, count:]], axis=1)

    key_square = jnp.zeros((1, rows), F32)
    smallest = jnp.full((1, wide), -floor_score, F32)
    for i in range(blocks // 2):
        for block in (2 * i, 2 * i + 1):
            ready(block)
            key_square = jnp.maximum(key_square, squares(k_buf[block * rows : (block + 1) * rows, :]))
        most = jnp.max(key_square, axis=1, keepdims=True)
        shift = jnp.sqrt(squares(q_buf[i * wide : (i + 1) * wide, :]) * most) * scale
        jobs = jobs_of(i)
        waiting = [score(i, job) for job in jobs[:AHEAD]]
        for n, (start, count, first, _) in enumerate(jobs):
            if n + AHEAD < len(jobs):
                waiting.append(score(i, jobs[n + AHEAD]))
            scores = waiting.pop(0)
            weights = jnp.exp2(scores * scale - shift[:, first:])
            total = jnp.sum(weights.reshape(count // 8, 8, wide - first), axis=0)
            update = mxu(vt_buf[:, start : start + count], weights.astype(BF16), PLAIN)
            if n == 0:
                acc_buf[i % 2] = update
                l_buf[i % 2] = total
            else:
                acc_buf[i % 2, :, first:] += update
                l_buf[i % 2, :, first:] += total
        total = jnp.sum(l_buf[i % 2], axis=0, keepdims=True)
        smallest = jnp.minimum(smallest, total)
        o_buf[i * wide : (i + 1) * wide, :] = (acc_buf[i % 2] / total).T.astype(BF16)

    @pl.when(jnp.min(smallest) < TOO_SMALL)
    def _():
        def one_query(i, carry):
            q_rows = pl.ds(pl.multiple_of(i * rows, rows), rows)
            m_buf[...] = jnp.full(m_buf.shape, floor_score, F32)
            l_buf[0, :, :rows] = jnp.zeros((8, rows), F32)
            acc_buf[0, :, :rows] = jnp.zeros((HEAD_DIM, rows), F32)

            def visit(j, masked):
                k_rows = pl.ds(pl.multiple_of(j * rows, rows), rows)
                scores = mxu(k_buf[k_rows, :], q_buf[q_rows, :], LAST)
                if masked:
                    scores = lower(scores)
                old = m_buf[:1, :]
                newest = jnp.maximum(old, jnp.max(scores, axis=0, keepdims=True) * scale)
                weights = jnp.exp2(scores * scale - newest)
                factor = jnp.exp2(old - newest)
                m_buf[:1, :] = newest
                l_buf[0, :, :rows] = l_buf[0, :, :rows] * factor + jnp.sum(
                    weights.reshape(rows // 8, 8, rows), axis=0
                )
                acc_buf[0, :, :rows] = acc_buf[0, :, :rows] * factor + mxu(
                    vt_buf[:, k_rows], weights.astype(BF16), PLAIN
                )

            def plain(j, inner):
                visit(j, False)
                return inner

            lax.fori_loop(0, i, plain, 0)
            visit(i, True)
            total = jnp.sum(l_buf[0, :, :rows], axis=0, keepdims=True)
            o_buf[q_rows, :] = (acc_buf[0, :, :rows] / total).T.astype(BF16)
            return carry

        lax.fori_loop(0, blocks, one_query, 0)

    writes = []
    for r in range(blocks):
        spot = pl.ds(pl.multiple_of((place ^ r) * rows, rows), rows)
        writes.append(pltpu.make_async_copy(o_buf.at[spot], outs[r], sems.at[r, 0]))
        writes[-1].start()
    for write in writes:
        write.wait()


def flash(place, sources):
    blocks, rows = len(sources), sources[0].shape[0] // 3
    total = blocks * rows
    pairs = total * (total + rows) // 2
    return pl.pallas_call(
        functools.partial(flash_kernel, blocks=blocks),
        in_specs=[pl.BlockSpec(memory_space=pltpu.SMEM)]
        + [pl.BlockSpec(memory_space=pl.ANY)] * blocks,
        out_specs=[pl.BlockSpec(memory_space=pl.ANY)] * blocks,
        out_shape=[jax.ShapeDtypeStruct((rows, HEAD_DIM), BF16)] * blocks,
        scratch_shapes=[
            pltpu.VMEM((total, HEAD_DIM), BF16),
            pltpu.VMEM((total, HEAD_DIM), BF16),
            pltpu.VMEM((total, HEAD_DIM), BF16),
            pltpu.VMEM((HEAD_DIM, total), BF16),
            pltpu.VMEM((total, HEAD_DIM), BF16),
            pltpu.VMEM((2, 8, 2 * rows), F32),
            pltpu.VMEM((2, HEAD_DIM, 2 * rows), F32),
            pltpu.VMEM((8, rows), F32),
            pltpu.SemaphoreType.DMA((blocks, 3)),
        ],
        compiler_params=WHOLE_VMEM,
        cost_estimate=pl.CostEstimate(
            flops=8 * pairs * HEAD_DIM, bytes_accessed=8 * total * HEAD_DIM, transcendentals=pairs
        ),
        name="flash",
    )(place, *sources)


def join_kernel(place_ref, *refs, blocks, heads):
    count = blocks * heads
    parts, out_ref, buf, sems = refs[:count], refs[-3], refs[-2], refs[-1]
    place = place_ref[0]
    reads, writes = [], []
    for n in range(count):
        reads.append(pltpu.make_async_copy(parts[n], buf.at[n], sems.at[0, n]))
        reads[-1].start()
    for n in range(count):
        column = pl.multiple_of(((place ^ (n % blocks)) * heads + n // blocks) * HEAD_DIM, HEAD_DIM)
        reads[n].wait()
        writes.append(
            pltpu.make_async_copy(buf.at[n], out_ref.at[:, pl.ds(column, HEAD_DIM)], sems.at[1, n])
        )
        writes[-1].start()
    for write in writes:
        write.wait()


def join(place, backs):
    heads, blocks = len(backs), len(backs[0])
    parts = [a for back in backs for a in back]
    rows = parts[0].shape[0]
    return pl.pallas_call(
        functools.partial(join_kernel, blocks=blocks, heads=heads),
        in_specs=[pl.BlockSpec(memory_space=pltpu.SMEM)]
        + [pl.BlockSpec(memory_space=pl.ANY)] * len(parts),
        out_specs=pl.BlockSpec(memory_space=pl.ANY),
        out_shape=jax.ShapeDtypeStruct((rows, blocks * heads * HEAD_DIM), BF16),
        scratch_shapes=[
            pltpu.VMEM((len(parts), rows, HEAD_DIM), BF16),
            pltpu.SemaphoreType.DMA((2, len(parts))),
        ],
        compiler_params=WHOLE_VMEM,
        cost_estimate=pl.CostEstimate(
            flops=0, bytes_accessed=4 * len(parts) * rows * HEAD_DIM, transcendentals=0
        ),
        name="join",
    )(place, *parts)


def exchange_body(
    gate_inner,
    gate_outer,
    hyena_value,
    decay_rate,
    residue,
    skip_gain,
    filter_index,
    query_rows,
    key_rows,
    value_rows,
    mesh,
):
    ctx_size, tp_size = mesh.shape["ctx"], mesh.shape["tp"]
    row_count, width_cols = query_rows.shape
    heads = width_cols // HEAD_DIM // ctx_size
    place = lax.axis_index("ctx")
    where = place.astype(jnp.int32).reshape(1)
    tiles = gate_inner.shape[1] // LANES

    def swap(a, r):
        return lax.ppermute(a, "ctx", [(i, i ^ r) for i in range(ctx_size)])

    order = list(SENDS) + [0]
    got, backs = [], []
    sent = query_rows
    lead = 1
    for h in range(heads):
        mine = [None] * ctx_size
        pieces = [order[:lead], order[lead:]] if h == 0 else [order]
        for some in pieces:
            packed = pack(where, (after(query_rows, sent), key_rows, value_rows), some, heads, h)
            sent = packed[0]
            for piece, r in zip(packed, some):
                mine[r] = swap(piece, r) if r else piece
        if h == 0:
            rate, local_residue = gathered_modes(
                decay_rate, residue, filter_index, tiles, tp_size, sent
            )
        got.append(mine)
    part, state = local_part(gate_inner, gate_outer, hyena_value, rate, local_residue, skip_gain)
    spot = jnp.stack([place.astype(jnp.int32), jnp.int32(row_count)])
    partner = swap(state, 1)
    (pair,) = state_call(pair_kernel, spot, rate, (state, partner), (BF16,))
    far = swap(pair, 2)
    for h in range(heads):
        results = flash(where, got[h])
        if h == heads - 2:
            far = after(far, results[0])
            before, total = state_call(gather_kernel, spot, rate, (partner, pair, far), (F32, BF16))
            other = swap(total, SPAN)
        back = list(results)
        for r in BACKS:
            back[r] = swap(results[r], r)
        backs.append(back)
    before = after(before, backs[-1][0])
    hyena_output = remote_part(where, part, gate_outer, rate, local_residue, before, other)
    backs[-1][0] = after(backs[-1][0], hyena_output)
    return (hyena_output, join(where, backs))


def row_steps(folded, members, handler, span_rows):
    total_rows = members[0].shape[0]
    block_count = total_rows // span_rows
    stacked = tuple(
        (member.reshape((block_count, span_rows) + member.shape[1:]) for member in members)
    )

    def advance(running, element):
        position, pieces = element
        return (handler(running, pieces, position * span_rows), None)

    folded, _ = lax.scan(advance, folded, (jnp.arange(block_count, dtype=jnp.int32), stacked))
    return folded


def gather_attention(query_rows, key_rows, value_rows):
    row_count, width_cols = query_rows.shape
    head_count = width_cols // HEAD_DIM
    queries = query_rows.reshape(row_count, head_count, HEAD_DIM)
    score_scale = 1.0 / math.sqrt(HEAD_DIM)
    own_rows = lax.axis_index("ctx") * row_count + jnp.arange(row_count, dtype=jnp.int32)

    def attend(folded, pieces, first_row):
        running_max, running_total, summed = folded
        block_rows = pieces[0].shape[0]
        keys_now = pieces[0].reshape(block_rows, head_count, HEAD_DIM)
        values_now = pieces[1].reshape(block_rows, head_count, HEAD_DIM)
        scores = (
            jnp.einsum("thd,shd->hts", queries, keys_now, preferred_element_type=jnp.float32)
            * score_scale
        )
        key_positions = first_row + jnp.arange(block_rows, dtype=jnp.int32)
        visible = own_rows[:, None] >= key_positions[None, :]
        masked = jnp.where(visible[None], scores, floor_score)
        newest = jnp.maximum(running_max, jnp.max(masked, axis=2))
        weights = jnp.where(visible[None], jnp.exp(scores - newest[:, :, None]), 0.0)
        factor = jnp.exp(running_max - newest)
        running_total = running_total * factor + jnp.sum(weights, axis=2)
        update = jnp.einsum(
            "hts,shd->thd",
            weights.astype(jnp.bfloat16),
            values_now,
            preferred_element_type=jnp.float32,
        )
        summed = summed * factor.T[:, :, None] + update
        return (newest, running_total, summed)

    initial = (
        jnp.full((head_count, row_count), floor_score, jnp.float32),
        jnp.zeros((head_count, row_count), jnp.float32),
        jnp.zeros((row_count, head_count, HEAD_DIM), jnp.float32),
    )
    _, running_total, summed = row_steps(
        initial,
        (
            lax.all_gather(key_rows, "ctx", axis=0, tiled=True),
            lax.all_gather(value_rows, "ctx", axis=0, tiled=True),
        ),
        attend,
        512,
    )
    result = summed / running_total.T[:, :, None]
    return result.reshape(row_count, width_cols).astype(jnp.bfloat16)


def solution(mesh):
    ctx_size, tp_size = mesh.shape["ctx"], mesh.shape["tp"]

    def body(
        gate_inner,
        gate_outer,
        hyena_value,
        decay_rate,
        residue,
        skip_gain,
        filter_index,
        query_rows,
        key_rows,
        value_rows,
    ):
        head_count = query_rows.shape[1] // HEAD_DIM
        if head_count % (2 * ctx_size) == 0 and ctx_size == 2 * SPAN:
            return exchange_body(
                gate_inner,
                gate_outer,
                hyena_value,
                decay_rate,
                residue,
                skip_gain,
                filter_index,
                query_rows,
                key_rows,
                value_rows,
                mesh,
            )
        attention_output = gather_attention(query_rows, key_rows, value_rows)
        tiles = gate_inner.shape[1] // LANES
        modes = gathered_modes(decay_rate, residue, filter_index, tiles, tp_size, None)
        hyena_output = hyena_plain(gate_inner, gate_outer, hyena_value, modes, skip_gain, ctx_size)
        return (hyena_output, attention_output)

    in_specs = (
        P("ctx", "tp"),
        P("ctx", "tp"),
        P("ctx", "tp"),
        P("tp", None),
        P("tp", None),
        P("tp"),
        P("tp"),
        P("ctx", "tp"),
        P("ctx", "tp"),
        P("ctx", "tp"),
    )
    out_specs = (P("ctx", "tp"), P("ctx", "tp"))
    return jax.shard_map(body, mesh=mesh, in_specs=in_specs, out_specs=out_specs, check_vma=False)
```
